32 devices in a mesh: blk: 16 (over z, y, core), rep: 2 (over x).
Axes of the slice: x: 2, y: 2, z: 4, core: 2. Of those that a mesh axis runs over, the one named last changes fastest.
Arguments:
- features: bfloat16 [32768, 256], P(('blk', 'rep')), may hold values from -6 to 6
- aggregated: bfloat16 [32768, 256], P(('blk', 'rep')), may hold values from -6 to 6
- out_grad: bfloat16 [32768, 256], P(('blk', 'rep')), may hold values from -6 to 6
- w_self: bfloat16 [256, 256], replicated, may hold values from -0.375 to 0.375
- w_neigh: bfloat16 [256, 256], replicated, may hold values from -0.375 to 0.375
- tiles: bfloat16 [16, 16, 8, 128, 128], P('blk'), may hold values from -0.0625 to 0.0625
- tile_rows: int32 [16, 16, 8], P('blk'), may hold values from 0 to 15
- tile_cols: int32 [16, 16, 8], P('blk'), may hold values from 0 to 15
- tile_counts: int32 [16, 16], P('blk'), may hold values from 0 to 8, as said below
Outputs:
- feature_grad: float32 [32768, 256], P(('blk', 'rep'))
- self_grad: float32 [256, 256], replicated
- neigh_grad: float32 [256, 256], replicated
The draws below stay inside these ranges and needn't reach their ends.
Inputs may be any that keep to these rules, and one draw needn't show every extreme that they name: `tile_counts`: at most 8; some pair of blocks uses all 8 slots; tiles, rows and columns of slots beyond the count carry no meaning.
All inputs are finite; a program needn't handle non-finite values.
Results may differ from the reference program's by a relative error of at most 0.00082.
Values may be sent and summed in bfloat16 or wider, within the bound.
A program may use at most 64 MiB of HBM per device.

```python
import jax
import jax.numpy as jnp
from jax import lax

F = 256
TILE = 128
TB = 16
SLOTS = 8
VERTS = 32768
N_BLK = 16


def draw_tile_counts(key, part):
    inner = jax.random.fold_in(key, 11)
    first_key, second_key = jax.random.split(inner)
    base = jax.random.randint(first_key, (N_BLK, N_BLK), SLOTS // 2, SLOTS + 1)
    ceiling = SLOTS - jnp.arange(N_BLK, dtype=jnp.int32) * (SLOTS // 2) // N_BLK
    counts = jnp.minimum(base, ceiling[:, None])
    column = jax.random.randint(second_key, (), 0, N_BLK)
    counts = counts.at[0, column].set(SLOTS)
    return counts.astype(jnp.int32)


def place_ends(result, own_key, low, largest):
    spot = [jax.random.randint(jax.random.fold_in(own_key, axis), (), 0, length) for axis, length in enumerate(result.shape)]
    longest = result.shape.index(max(result.shape))
    next_to = spot[:longest] + [(spot[longest] + 1) % result.shape[longest]] + spot[longest + 1:]
    return result.at[tuple(spot)].set(low).at[tuple(next_to)].set(largest)


def shard_levels(own_key, extent, cuts, low, top_value):
    factor_of, own = 1.0, jax.random.fold_in(own_key, 6)
    for dim, shards_of in cuts:
        draws = jnp.exp(jax.random.uniform(jax.random.fold_in(own, dim), (shards_of,), jnp.float32, low / len(cuts), top_value / len(cuts)))
        factor_of = factor_of * jnp.repeat(draws, extent[dim] // shards_of).reshape([-1 if axis == dim else 1 for axis in range(len(extent))])
    return factor_of


def scatter_about(stream_key, dims, deviation, reach, cuts=(), held_as=jnp.bfloat16):
    drawn = jax.random.normal(stream_key, dims, jnp.float32) * deviation
    if len(cuts) > 0:
        drawn = shard_levels(stream_key, dims, cuts, -0.22, 0.18) * drawn
    return jnp.clip(drawn, min=-reach, max=reach).astype(held_as)


def setup_inputs(seed: int = 0) -> dict:
    arg_keys = jax.random.split(jax.random.key(seed), 10)
    return {
        "features": scatter_about(arg_keys[0], (VERTS, F), 1.0, 6.0, ((0, 32),)),
        "aggregated": scatter_about(arg_keys[1], (VERTS, F), 1.0, 6.0, ((0, 32),)),
        "out_grad": scatter_about(arg_keys[2], (VERTS, F), 1.0, 6.0, ((0, 32),)),
        "w_self": scatter_about(arg_keys[3], (F, F), F ** -0.5, 0.375),
        "w_neigh": scatter_about(arg_keys[4], (F, F), F ** -0.5, 0.375),
        "tiles": scatter_about(arg_keys[5], (N_BLK, N_BLK, SLOTS, TILE, TILE), (TILE * SLOTS * N_BLK // 2) ** -0.5, 0.0625, ((0, 16),)),
        "tile_rows": place_ends(jax.random.randint(arg_keys[6], (N_BLK, N_BLK, SLOTS), 0, TB), jax.random.fold_in(arg_keys[6], 1), 0, TB - 1).astype(jnp.int32),
        "tile_cols": place_ends(jax.random.randint(arg_keys[7], (N_BLK, N_BLK, SLOTS), 0, TB), jax.random.fold_in(arg_keys[7], 1), 0, TB - 1).astype(jnp.int32),
        "tile_counts": draw_tile_counts(jax.random.fold_in(arg_keys[9], 71), 0),
    }


def reference(features, aggregated, out_grad, w_self, w_neigh, tiles, tile_rows, tile_cols, tile_counts):
    message = jnp.dot(out_grad, w_neigh.T, preferred_element_type=jnp.float32).astype(jnp.bfloat16)
    pieces_all = message.reshape(N_BLK * TB, TILE, F)

    def one_block(block_index):
        blocks = tiles[block_index].reshape(N_BLK * SLOTS, TILE, TILE).astype(jnp.float32)
        index = (jnp.arange(N_BLK, dtype=jnp.int32)[:, None] * TB + tile_cols[block_index]).reshape(-1).astype(jnp.int32)
        pieces = pieces_all[index].astype(jnp.float32)
        products = jnp.einsum("kpq,kqf->kpf", blocks, pieces)
        live = (jnp.arange(SLOTS, dtype=jnp.int32)[None, :] < tile_counts[block_index][:, None]).reshape(-1)
        products = jnp.where(live[:, None, None], products, jnp.zeros_like(products))
        start = jnp.zeros((TB, TILE, F), products.dtype)
        return start.at[tile_rows[block_index].reshape(-1)].add(products)

    spread = lax.map(one_block, jnp.arange(N_BLK, dtype=jnp.int32)).reshape(N_BLK * TB * TILE, F)
    feature_grad = jnp.dot(out_grad, w_self.T, preferred_element_type=jnp.float32) + spread
    scale = VERTS ** -0.5
    contract = (((0,), (0,)), ((), ()))
    self_grad = lax.dot_general(features, out_grad, contract, preferred_element_type=jnp.float32) * scale
    neigh_grad = lax.dot_general(aggregated, out_grad, contract, preferred_element_type=jnp.float32) * scale
    return (feature_grad, self_grad, neigh_grad)
```

```python
import functools

import jax
import jax.numpy as jnp
from jax import lax
from jax.experimental import pallas as pl
from jax.experimental.pallas import tpu as pltpu
from jax.sharding import PartitionSpec as P

MESH = pl.DeviceIdType.MESH
CORES, ROWS_Y = 2, 2


PIECES = 2


def positions(line):
    last = 2 * (line - 1) + 1
    own = lambda d, w: 2 * (d - 1) + 1 + w if d else w
    ends = {}
    for d in range(line):
        ends[d, 0, 0] = own(d, 1) + 0.5
        ends[d, 1, 0] = 2.5 if d == 0 else min(own(d, 1) + 3, last + (d == line - 1) * 0.8) + 0.1
    for d in range(line):
        for other in range(2):
            ends[d, other, 1] = ends[d, other, 0] + (0.1 if ends[d, other, 0] > last else 0.95)
    return ends


def layer_kernel(
    blocks,
    copies,
    scale,
    rows_ref,
    cols_ref,
    counts_ref,
    features_ref,
    aggregated_ref,
    grad_ref,
    w_self_ref,
    w_neigh_ref,
    tiles_ref,
    base_ref,
    got_ref,
    sum_ref,
    rows_v,
    counts_v,
    rows_s,
    cols_s,
    counts_s,
    features_v,
    aggregated_v,
    grad_v,
    w_self_v,
    w_neigh_v,
    tiles_v,
    g,
    across,
    current,
    chain,
    links_v,
    links_s,
    base_v,
    back,
    terms,
    from_core,
    half_sum,
    from_x,
    quarter_sum,
    from_plane,
    total,
    local_sem,
    send_sem,
    recv_sem,
    x_send,
    back_send,
    back_recv,
    core_send,
    core_recv,
    pair_send,
    pair_recv,
    plane_send,
    plane_recv,
):
    b = lax.axis_index("blk")
    r = lax.axis_index("rep")
    plane = CORES * ROWS_Y
    line = blocks // plane
    z, y, c = b // plane, (b // CORES) % ROWS_Y, b % CORES
    near_x = (b, 1 - r)
    near_core = (z * plane + y * CORES + (1 - c), r)
    near_y = (z * plane + (1 - y) * CORES + c, r)
    up, down = (b + plane, r), (b - plane, r)
    has_up, has_down = z < line - 1, z > 0
    never = z < 0
    always = z >= 0
    pieces, piece_rows, width = g.shape[2:]
    slots, side = tiles_v.shape[1], tiles_v.shape[2]
    share_tiles = pieces * piece_rows // side
    seats = line * ROWS_Y
    seat = z * ROWS_Y + y
    end_of = lambda zz: (zz == 0) | (zz == line - 1)

    def local(src, dst, n):
        return pltpu.make_async_copy(src, dst, local_sem.at[n])

    loads = [
        local(grad_ref, grad_v, 0),
        local(w_neigh_ref, w_neigh_v, 1),
        local(features_ref, features_v, 2),
        local(aggregated_ref, aggregated_v, 3),
        local(rows_ref, rows_v, 4),
        local(counts_ref, counts_v, 5),
        local(rows_ref, rows_s, 6),
        local(cols_ref, cols_s, 7),
        local(counts_ref, counts_s, 8),
        local(w_self_ref, w_self_v, 9),
        local(tiles_ref, tiles_v, 10),
    ]
    for load in loads:
        load.start()

    barrier = pltpu.get_barrier_semaphore()

    def greet(device):
        pl.semaphore_signal(barrier, inc=1, device_id=device, device_id_type=MESH)

    def seat_device(step):
        other = (seat + step) % seats
        return other, ((other // ROWS_Y) * plane + (other % ROWS_Y) * CORES + c, r)

    greet(near_x)
    greet(near_core)

    @pl.loop(1, seats)
    def _(step):
        greet(seat_device(step)[1])

    loads[0].wait()
    loads[1].wait()

    def message(which, h):
        return lax.dot_general(
            grad_v[pl.ds(h * piece_rows, piece_rows), :],
            w_neigh_v[pl.ds(pl.multiple_of(which * width, width), width), :],
            (((1,), (1,)), ((), ())),
            preferred_element_type=jnp.float32,
        ).astype(g.dtype)

    for h in range(pieces):
        g[b, r, h] = message(r, h)
    for h in range(pieces):
        across[h] = message(1 - r, h)

    pl.semaphore_wait(barrier, 2 + seats - 1)

    def send(block, share, h, way, device):
        return pltpu.make_async_remote_copy(
            src_ref=g.at[block, share, h],
            dst_ref=g.at[block, share, h],
            send_sem=send_sem.at[way, block, share, h],
            recv_sem=recv_sem.at[block, share, h],
            device_id=device,
            device_id_type=MESH,
        )

    def x_copy(h):
        return pltpu.make_async_remote_copy(
            src_ref=across.at[h],
            dst_ref=g.at[b, r, h],
            send_sem=x_send.at[h],
            recv_sem=recv_sem.at[b, r, h],
            device_id=near_x,
            device_id_type=MESH,
        )

    def arrived(block, share, h):
        send(block, share, h, 3, near_core).wait_recv()

    def pass_on(block, share, h, go_up, go_down, go_y):
        @pl.when(go_up)
        def _():
            send(block, share, h, 0, up).start()

        @pl.when(go_down)
        def _():
            send(block, share, h, 1, down).start()

        @pl.when(go_y)
        def _():
            send(block, share, h, 2, near_y).start()

        send(block, share, h, 3, near_core).start()

    def share_of(which):
        return r if which == 0 else 1 - r

    def there(zz):
        return (zz >= 0) & (zz < line)

    def own_line(d, which):
        share = share_of(which)

        @pl.loop(0, pieces)
        def _(h):
            for sign in (-1, 1):
                zz = z + sign * d

                @pl.when(there(zz))
                def _():
                    block = zz * plane + y * CORES + c
                    arrived(block, share, h)
                    pass_on(
                        block,
                        share,
                        h,
                        has_up if sign < 0 else never,
                        has_down if sign > 0 else never,
                        jnp.logical_not(end_of(zz)) if which else always,
                    )

    def from_across():
        @pl.loop(0, pieces)
        def _(h):
            arrived(b, 1 - r, h)
            pass_on(b, 1 - r, h, has_up, has_down, always)

    def from_y(d, which):
        share = share_of(which)

        @pl.loop(0, pieces)
        def _(h):
            for sign in (-1, 1) if d else (0,):
                zz = z + sign * d
                wanted = there(zz)
                if which and d:
                    wanted = wanted & jnp.logical_not(end_of(zz))

                @pl.when(wanted)
                def _():
                    block = zz * plane + (1 - y) * CORES + c
                    arrived(block, share, h)
                    onward = which == 1 and d == 0
                    pass_on(
                        block,
                        share,
                        h,
                        has_up & (z == 0) if onward else never,
                        has_down & (z == line - 1) if onward else never,
                        never,
                    )

    def end_line(d):
        share = share_of(1)

        @pl.loop(0, pieces)
        def _(h):
            for sign in (-1, 1):
                zz = z + sign * d

                @pl.when(there(zz) & end_of(zz))
                def _():
                    block = zz * plane + (1 - y) * CORES + c
                    arrived(block, share, h)
                    pass_on(
                        block,
                        share,
                        h,
                        has_up if sign < 0 else never,
                        has_down if sign > 0 else never,
                        never,
                    )

    ends = positions(line)
    order = sorted(ends, key=lambda group: (ends[group], group))
    starts, count = {}, 0
    for group in order:
        starts[group] = count
        count += 2 if group[0] else 1
    nothing = count * slots

    def block_of(zz, other_y, other_core):
        yy = 1 - y if other_y else y
        cc = 1 - c if other_core else c
        return zz * plane + yy * CORES + cc

    def chain_links():
        for n in (4, 5, 6, 7, 8):
            loads[n].wait()
        slot = lax.broadcasted_iota(jnp.int32, rows_v.shape, 0)
        lane = lax.broadcasted_iota(jnp.int32, rows_v.shape, 1)
        wanted = jnp.where(slot < counts_v[...], rows_v[...], -2)
        candidates = [
            (starts[group] + i, group, sign)
            for group in order
            for i, sign in enumerate((-1, 1) if group[0] else (0,))
        ]
        own = slot
        found = []
        for index, (d, other_y, other_core), sign in candidates:
            zz = z + sign * d
            ok = there(zz)
            block = jnp.where(ok, block_of(zz, other_y, other_core), 0)
            own = jnp.where((lane == block) & ok, slot + index * slots, own)
            found.append((index * slots, block, ok))

        def step(k, carry):
            before, last = carry
            for first, block, ok in found:
                ok = ok & (k < counts_s[0, block])
                row = jnp.where(ok, rows_s[k, block], -1)
                key = first + k
                before = jnp.where((wanted == row) & (own > key), jnp.maximum(before, key), before)
                last = jnp.where(lane == row, jnp.maximum(last, key), last)
            return before, last

        none = jnp.full(rows_v.shape, -1, jnp.int32)
        before, last = lax.fori_loop(0, slots, step, (none, none))
        links_v[0] = jnp.where(before < 0, nothing, before)
        links_v[1] = jnp.where(last < 0, nothing, last)
        chain[nothing] = jnp.zeros(chain.shape[1:], chain.dtype)

    def links_copy():
        return local(links_v, links_s, 11)

    def multiply(group):
        d, other_y, other_core = group
        first = starts[group]

        def one(i):
            zz = z + (2 * i - 1) * d

            @pl.when(there(zz))
            def _():
                block = block_of(zz, other_y, other_core)
                if other_core:

                    @pl.loop(0, pieces)
                    def _(h):
                        for share in range(copies):
                            arrived(block, share, h)

                seat_of = first + i
                current[seat_of] = g[block].reshape(current.shape[1:])
                products = []
                for k in range(slots):
                    products.append(
                        jnp.dot(
                            tiles_v[block, k],
                            current[seat_of, cols_s[k, block]],
                            preferred_element_type=jnp.float32,
                        )
                    )
                for k in range(slots):
                    chain[seat_of * slots + k] = products[k] + chain[links_s[0, k, block]]

        if d:

            @pl.loop(0, 2)
            def _(i):
                one(i)
        else:
            one(0)

    out_width = total.shape[1]
    half, quarter = total.shape[0] // 2, total.shape[0] // 4
    part = quarter // seats

    def core_copy():
        return pltpu.make_async_remote_copy(
            src_ref=terms.at[pl.ds((1 - c) * half, half)],
            dst_ref=from_core,
            send_sem=core_send.at[0],
            recv_sem=core_recv.at[0],
            device_id=near_core,
            device_id_type=MESH,
        )

    def pair_copy():
        return pltpu.make_async_remote_copy(
            src_ref=half_sum.at[pl.ds((1 - r) * quarter, quarter)],
            dst_ref=from_x,
            send_sem=pair_send.at[0],
            recv_sem=pair_recv.at[0],
            device_id=near_x,
            device_id_type=MESH,
        )

    def part_copy(step, slot):
        other, device = seat_device(step)
        return pltpu.make_async_remote_copy(
            src_ref=quarter_sum.at[pl.ds(other * part, part)],
            dst_ref=from_plane.at[slot],
            send_sem=plane_send.at[0, other],
            recv_sem=plane_recv.at[0, slot],
            device_id=device,
            device_id_type=MESH,
        )

    def share_copy(step, owner):
        other, device = seat_device(step)
        where = pl.ds(c * half + r * quarter + owner * part, part)
        return pltpu.make_async_remote_copy(
            src_ref=total.at[where],
            dst_ref=total.at[where],
            send_sem=plane_send.at[1, other],
            recv_sem=plane_recv.at[1, owner],
            device_id=device,
            device_id_type=MESH,
        )

    def pair_back(rr):
        where = pl.ds(c * half + rr * quarter, quarter)
        return pltpu.make_async_remote_copy(
            src_ref=total.at[where],
            dst_ref=total.at[where],
            send_sem=pair_send.at[1],
            recv_sem=pair_recv.at[1],
            device_id=near_x,
            device_id_type=MESH,
        )

    def core_back(cc):
        where = pl.ds(cc * half, half)
        return pltpu.make_async_remote_copy(
            src_ref=total.at[where],
            dst_ref=total.at[where],
            send_sem=core_send.at[1],
            recv_sem=core_recv.at[1],
            device_id=near_core,
            device_id_type=MESH,
        )

    def make_terms():
        loads[2].wait()
        loads[3].wait()
        for n, operand in enumerate((features_v, aggregated_v)):
            terms[n * half : (n + 1) * half, :] = lax.dot_general(
                operand[...],
                grad_v[...],
                (((0,), (0,)), ((), ())),
                preferred_element_type=jnp.float32,
            )
        core_copy().start()

    def over_cores():
        core_copy().wait_recv()
        half_sum[...] = terms[pl.ds(pl.multiple_of(c * half, half), half), :] + from_core[...]
        pair_copy().start()

    def over_pair():
        pair_copy().wait_recv()
        quarter_sum[...] = (
            half_sum[pl.ds(pl.multiple_of(r * quarter, quarter), quarter), :] + from_x[...]
        )

        @pl.loop(1, seats)
        def _(step):
            part_copy(step, seat).start()

    def over_plane():
        from_plane[seat] = quarter_sum[pl.ds(pl.multiple_of(seat * part, part), part), :]

        @pl.loop(1, seats)
        def _(step):
            part_copy(step, seat_device(step)[0]).wait_recv()

        where = pl.ds(pl.multiple_of(c * half + r * quarter + seat * part, part), part)
        total[where, :] = jnp.sum(from_plane[...], axis=0) * scale

        @pl.loop(1, seats)
        def _(step):
            share_copy(step, seat).start()

    def back_over_pair():
        @pl.loop(1, seats)
        def _(step):
            share_copy(step, seat_device(step)[0]).wait_recv()

        pair_back(r).start()

    def back_over_cores():
        pair_back(1 - r).wait_recv()
        core_back(c).start()

    def self_part():
        loads[9].wait()

        @pl.loop(0, pieces)
        def _(h):
            where = pl.ds(pl.multiple_of(h * piece_rows, piece_rows), piece_rows)
            base_v[where, :] = lax.dot_general(
                grad_v[where, :],
                w_self_v[...],
                (((1,), (1,)), ((), ())),
                preferred_element_type=jnp.float32,
            )

    for h in range(pieces):
        x_copy(h).start()
        pass_on(b, r, h, has_up, has_down, always)

    last = 2 * (line - 1) + 1
    events = [
        (0.1, make_terms),
        (0.2, chain_links),
        (0.3, lambda: links_copy().start()),
        (0.9, over_cores),
        (1.0, from_across),
        (1.45, lambda: (links_copy().wait(), loads[10].wait())),
        (1.9, over_pair),
        (2.9, self_part),
        (3.9, over_plane),
        (5.9, back_over_pair),
        (6.7, back_over_cores),
    ]
    for which in range(2):
        events.append((1.1 + which, functools.partial(from_y, 0, which)))
        for d in range(1, line):
            when = 2 * (d - 1) + 1 + which
            events.append((when, functools.partial(own_line, d, which)))
            if which == 0 or d < line - 1:
                late = min(when + 3, last + (d == line - 1) * 0.8) + 0.05
                events.append((late, functools.partial(from_y, d, which)))
    for d in range(1, line):
        events.append((2 * d + 1 + (d == line - 1) * 0.8, functools.partial(end_line, d)))
    for group in order:
        events.append((ends[group], functools.partial(multiply, group)))
    for _, event in sorted(events, key=lambda pair: pair[0]):
        event()

    def back_copy():
        return pltpu.make_async_remote_copy(
            src_ref=back,
            dst_ref=got_ref,
            send_sem=back_send,
            recv_sem=back_recv,
            device_id=near_x,
            device_id_type=MESH,
        )

    for t in range(share_tiles):
        row = (1 - r) * share_tiles + t
        back[t * side : (t + 1) * side, :] = chain[links_s[1, 0, row]].astype(back.dtype)
    own_half = pl.ds(pl.multiple_of(r * width, width), width)
    for t in range(share_tiles):
        if t == 1:
            back_copy().start()
        row = r * share_tiles + t
        base_v[t * side : (t + 1) * side, own_half] += chain[links_s[1, 0, row]]
    base_copy = local(base_v, base_ref, 12)
    base_copy.start()
    core_back(1 - c).wait_recv()
    sum_copy = local(total, sum_ref, 13)
    sum_copy.start()

    core_copy().wait_send()
    pair_copy().wait_send()
    pair_back(r).wait_send()
    core_back(c).wait_send()

    @pl.loop(1, seats)
    def _(step):
        part_copy(step, seat).wait_send()
        share_copy(step, seat).wait_send()

    @pl.loop(0, pieces)
    def _(h):
        x_copy(h).wait_send()

        @pl.loop(0, line)
        def _(zz):
            for which in range(2):
                share = share_of(which)
                block = zz * plane + y * CORES + c
                beyond = zz * plane + (1 - y) * CORES + c
                special = end_of(zz) if which else never
                goes_up = (zz <= z) & has_up
                goes_down = (zz >= z) & has_down

                @pl.when(goes_up)
                def _():
                    send(block, share, h, 0, up).wait_send()

                @pl.when(goes_down)
                def _():
                    send(block, share, h, 1, down).wait_send()

                @pl.when(jnp.logical_not(special) | (zz == z))
                def _():
                    send(block, share, h, 2, near_y).wait_send()

                send(block, share, h, 3, near_core).wait_send()

                @pl.when(special & goes_up)
                def _():
                    send(beyond, share, h, 0, up).wait_send()

                @pl.when(special & goes_down)
                def _():
                    send(beyond, share, h, 1, down).wait_send()

                send(beyond, share, h, 3, near_core).wait_send()

    sum_copy.wait()
    base_copy.wait()
    back_copy().wait_send()
    back_copy().wait_recv()


def layer(rows, cols, counts, features, aggregated, grad, w_self, w_neigh, tiles, scale, blocks, copies):
    share_rows, width = grad.shape
    half = width // copies
    _, slots, side, _ = tiles.shape
    line = blocks // (CORES * ROWS_Y)
    seats = line * ROWS_Y
    piece_rows = share_rows // PIECES
    count = 2 * CORES * (2 * line - 1)
    bf16, f32, i32 = jnp.bfloat16, jnp.float32, jnp.int32
    dma = pltpu.SemaphoreType.DMA
    operands = (rows, cols, counts, features, aggregated, grad, w_self, w_neigh, tiles)
    return pl.pallas_call(
        functools.partial(layer_kernel, blocks, copies, scale),
        out_shape=(
            jax.ShapeDtypeStruct((share_rows, width), f32),
            jax.ShapeDtypeStruct((share_rows, half), bf16),
            jax.ShapeDtypeStruct((2 * width, width), f32),
        ),
        in_specs=[pl.BlockSpec(memory_space=pl.ANY)] * 9,
        out_specs=(pl.BlockSpec(memory_space=pl.ANY),) * 3,
        scratch_shapes=[
            pltpu.VMEM(rows.shape, i32),
            pltpu.VMEM(counts.shape, i32),
            pltpu.SMEM(rows.shape, i32),
            pltpu.SMEM(cols.shape, i32),
            pltpu.SMEM(counts.shape, i32),
            pltpu.VMEM(features.shape, bf16),
            pltpu.VMEM(aggregated.shape, bf16),
            pltpu.VMEM(grad.shape, bf16),
            pltpu.VMEM(w_self.shape, bf16),
            pltpu.VMEM(w_neigh.shape, bf16),
            pltpu.VMEM(tiles.shape, bf16),
            pltpu.VMEM((blocks, copies, PIECES, piece_rows, half), bf16),
            pltpu.VMEM((PIECES, piece_rows, half), bf16),
            pltpu.VMEM((count, copies * share_rows // side, side, half), bf16),
            pltpu.VMEM((count * slots + 1, side, half), f32),
            pltpu.VMEM((2, *rows.shape), i32),
            pltpu.SMEM((2, *rows.shape), i32),
            pltpu.VMEM((share_rows, width), f32),
            pltpu.VMEM((share_rows, half), bf16),
            pltpu.VMEM((2 * width, width), f32),
            pltpu.VMEM((width, width), f32),
            pltpu.VMEM((width, width), f32),
            pltpu.VMEM((width // 2, width), f32),
            pltpu.VMEM((width // 2, width), f32),
            pltpu.VMEM((seats, width // 2 // seats, width), f32),
            pltpu.VMEM((2 * width, width), f32),
            dma((14,)),
            dma((4, blocks, copies, PIECES)),
            dma((blocks, copies, PIECES)),
            dma((PIECES,)),
            dma,
            dma,
            dma((2,)),
            dma((2,)),
            dma((2,)),
            dma((2,)),
            dma((2, seats)),
            dma((2, seats)),
        ],
        compiler_params=pltpu.CompilerParams(collective_id=0, has_side_effects=True, vmem_limit_bytes=48 << 20),
    )(*(pltpu.with_memory_space_constraint(operand, pltpu.HBM) for operand in operands))


def by_columns(
    features, aggregated, out_grad, w_self, w_neigh, tiles, tile_rows, tile_cols, tile_counts
):
    blocks, copies = lax.axis_size("blk"), lax.axis_size("rep")
    r = lax.axis_index("rep")
    rows, width = out_grad.shape
    half = width // copies
    scale = (rows * blocks * copies) ** (-0.5)
    base, got, sums = layer(
        tile_rows[0].T,
        tile_cols[0].T,
        tile_counts,
        features,
        aggregated,
        out_grad,
        w_self,
        w_neigh,
        tiles[0],
        scale,
        blocks,
        copies,
    )
    other = (jnp.arange(width, dtype=jnp.int32) // half)[None, :] != r
    got = jnp.concatenate([got, got], axis=1).astype(jnp.float32)
    feature_grad = base + jnp.where(other, got, jnp.zeros_like(got))
    return (feature_grad, sums[:width], sums[width:])


def on_device(
    features, aggregated, out_grad, w_self, w_neigh, tiles, tile_rows, tile_cols, tile_counts
):
    block_total = lax.axis_size("blk")
    copies = lax.axis_size("rep")
    replica = lax.axis_index("rep")
    width = out_grad.shape[1]
    side = tiles.shape[-1]
    slots_total = tiles.shape[2]
    share = jnp.dot(out_grad, w_neigh.T, preferred_element_type=jnp.float32).astype(jnp.bfloat16)
    whole = lax.all_gather(share, "rep", axis=0, tiled=True)
    block_rows = whole.shape[0]
    tiles_side = block_rows // side
    pieces_whole = whole.reshape(tiles_side, side, width)
    per_copy = (slots_total + copies - 1) // copies
    slot_ids = replica + copies * jnp.arange(per_copy, dtype=jnp.int32)
    valid = slot_ids < slots_total
    safe = jnp.minimum(slot_ids, slots_total - 1)
    wanted = jnp.take(tile_cols[0], safe, axis=1)
    found = pieces_whole[lax.all_to_all(wanted, "blk", split_axis=0, concat_axis=0, tiled=True)]
    fetched = lax.all_to_all(found, "blk", split_axis=0, concat_axis=0, tiled=True)
    chosen_tiles = jnp.take(tiles[0], safe, axis=1)
    products = jnp.einsum(
        "ikpq,ikqf->ikpf", chosen_tiles, fetched, preferred_element_type=jnp.float32
    )
    live = valid[None, :] & (slot_ids[None, :] < tile_counts[0][:, None])
    products = jnp.where(live[:, :, None, None], products, jnp.zeros_like(products))
    target_rows = jnp.take(tile_rows[0], safe, axis=1).reshape(-1)
    accumulated = jnp.zeros((tiles_side, side, width), jnp.float32)
    accumulated = accumulated.at[target_rows].add(products.reshape(-1, side, width))
    flat = accumulated.reshape(block_rows, width)
    self_part = jnp.dot(out_grad, w_self.T, preferred_element_type=jnp.float32)
    contract = (((0,), (0,)), ((), ()))
    terms_self = lax.dot_general(features, out_grad, contract, preferred_element_type=jnp.float32)
    terms_neigh = lax.dot_general(
        aggregated, out_grad, contract, preferred_element_type=jnp.float32
    )
    scale = (out_grad.shape[0] * block_total * copies) ** (-0.5)
    spread_share = lax.psum_scatter(flat, "rep", scatter_dimension=0, tiled=True)
    self_sum, neigh_sum = lax.psum((terms_self, terms_neigh), ("blk", "rep"))
    return (spread_share + self_part, self_sum * scale, neigh_sum * scale)


def solution(mesh):
    blocks, copies = mesh.shape["blk"], mesh.shape["rep"]
    by_pairs = copies == 2 and blocks % (CORES * ROWS_Y) == 0
    placed = (
        P(("blk", "rep"), None),
        P(("blk", "rep"), None),
        P(("blk", "rep"), None),
        P(),
        P(),
        P("blk", None, None, None, None),
        P("blk", None, None),
        P("blk", None, None),
        P("blk", None),
    )
    return jax.shard_map(
        by_columns if by_pairs else on_device,
        mesh=mesh,
        in_specs=placed,
        out_specs=(P(("blk", "rep"), None), P(), P()),
        check_vma=False,
    )
```

```python
import functools

import jax
import jax.numpy as jnp
from jax import lax
from jax.experimental import pallas as pl
from jax.experimental.pallas import tpu as pltpu
from jax.sharding import PartitionSpec as P

MESH = pl.DeviceIdType.MESH
CORES, ROWS_Y = 2, 2


PIECES = 2


def positions(line):
    last = 2 * (line - 1) + 1
    own = lambda d, w: 2 * (d - 1) + 1 + w if d else w
    ends = {}
    for d in range(line):
        ends[d, 0, 0] = own(d, 1) + 0.5
        ends[d, 1, 0] = 2.5 if d == 0 else min(own(d, 1) + 3, last + (d == line - 1) * 0.8) + 0.1
    for d in range(line):
        for other in range(2):
            ends[d, other, 1] = ends[d, other, 0] + (0.1 if ends[d, other, 0] > last else 0.95)
    return ends


def layer_kernel(
    blocks,
    copies,
    scale,
    rows_ref,
    cols_ref,
    counts_ref,
    features_ref,
    aggregated_ref,
    grad_ref,
    w_self_ref,
    w_neigh_ref,
    tiles_ref,
    base_ref,
    got_ref,
    sum_ref,
    rows_v,
    counts_v,
    rows_s,
    cols_s,
    counts_s,
    features_v,
    aggregated_v,
    grad_v,
    w_self_v,
    w_neigh_v,
    tiles_v,
    g,
    across,
    current,
    chain,
    links_v,
    links_s,
    base_v,
    back,
    terms,
    from_core,
    half_sum,
    from_x,
    quarter_sum,
    from_plane,
    total,
    local_sem,
    send_sem,
    recv_sem,
    x_send,
    back_send,
    back_recv,
    core_send,
    core_recv,
    pair_send,
    pair_recv,
    plane_send,
    plane_recv,
):
    b = lax.axis_index("blk")
    r = lax.axis_index("rep")
    plane = CORES * ROWS_Y
    line = blocks // plane
    z, y, c = b // plane, (b // CORES) % ROWS_Y, b % CORES
    near_x = (b, 1 - r)
    near_core = (z * plane + y * CORES + (1 - c), r)
    near_y = (z * plane + (1 - y) * CORES + c, r)
    up, down = (b + plane, r), (b - plane, r)
    has_up, has_down = z < line - 1, z > 0
    never = z < 0
    always = z >= 0
    pieces, piece_rows, width = g.shape[2:]
    slots, side = tiles_v.shape[1], tiles_v.shape[2]
    share_tiles = pieces * piece_rows // side
    seats = line * ROWS_Y
    seat = z * ROWS_Y + y
    end_of = lambda zz: (zz == 0) | (zz == line - 1)

    def local(src, dst, n):
        return pltpu.make_async_copy(src, dst, local_sem.at[n])

    loads = [
        local(grad_ref, grad_v, 0),
        local(w_neigh_ref, w_neigh_v, 1),
        local(features_ref, features_v, 2),
        local(aggregated_ref, aggregated_v, 3),
        local(rows_ref, rows_v, 4),
        local(counts_ref, counts_v, 5),
        local(rows_ref, rows_s, 6),
        local(cols_ref, cols_s, 7),
        local(counts_ref, counts_s, 8),
        local(w_self_ref, w_self_v, 9),
        local(tiles_ref, tiles_v, 10),
    ]
    for load in loads:
        load.start()

    barrier = pltpu.get_barrier_semaphore()

    def greet(device):
        pl.semaphore_signal(barrier, inc=1, device_id=device, device_id_type=MESH)

    def seat_device(step):
        other = (seat + step) % seats
        return other, ((other // ROWS_Y) * plane + (other % ROWS_Y) * CORES + c, r)

    greet(near_x)
    greet(near_core)

    @pl.loop(1, seats)
    def _(step):
        greet(seat_device(step)[1])

    loads[0].wait()
    loads[1].wait()

    def message(which, h):
        return lax.dot_general(
            grad_v[pl.ds(h * piece_rows, piece_rows), :],
            w_neigh_v[pl.ds(pl.multiple_of(which * width, width), width), :],
            (((1,), (1,)), ((), ())),
            preferred_element_type=jnp.float32,
        ).astype(g.dtype)

    for h in range(pieces):
        g[b, r, h] = message(r, h)
    for h in range(pieces):
        across[h] = message(1 - r, h)

    pl.semaphore_wait(barrier, 2 + seats - 1)

    def send(block, share, h, way, device):
        return pltpu.make_async_remote_copy(
            src_ref=g.at[block, share, h],
            dst_ref=g.at[block, share, h],
            send_sem=send_sem.at[way, block, share, h],
            recv_sem=recv_sem.at[block, share, h],
            device_id=device,
            device_id_type=MESH,
        )

    def x_copy(h):
        return pltpu.make_async_remote_copy(
            src_ref=across.at[h],
            dst_ref=g.at[b, r, h],
            send_sem=x_send.at[h],
            recv_sem=recv_sem.at[b, r, h],
            device_id=near_x,
            device_id_type=MESH,
        )

    def arrived(block, share, h):
        send(block, share, h, 3, near_core).wait_recv()

    def pass_on(block, share, h, go_up, go_down, go_y):
        @pl.when(go_up)
        def _():
            send(block, share, h, 0, up).start()

        @pl.when(go_down)
        def _():
            send(block, share, h, 1, down).start()

        @pl.when(go_y)
        def _():
            send(block, share, h, 2, near_y).start()

        send(block, share, h, 3, near_core).start()

    def share_of(which):
        return r if which == 0 else 1 - r

    def there(zz):
        return (zz >= 0) & (zz < line)

    def own_line(d, which):
        share = share_of(which)

        @pl.loop(0, pieces)
        def _(h):
            for sign in (-1, 1):
                zz = z + sign * d

                @pl.when(there(zz))
                def _():
                    block = zz * plane + y * CORES + c
                    arrived(block, share, h)
                    pass_on(
                        block,
                        share,
                        h,
                        has_up if sign < 0 else never,
                        has_down if sign > 0 else never,
                        jnp.logical_not(end_of(zz)) if which else always,
                    )

    def from_across():
        @pl.loop(0, pieces)
        def _(h):
            arrived(b, 1 - r, h)
            pass_on(b, 1 - r, h, has_up, has_down, always)

    def from_y(d, which):
        share = share_of(which)

        @pl.loop(0, pieces)
        def _(h):
            for sign in (-1, 1) if d else (0,):
                zz = z + sign * d
                wanted = there(zz)
                if which and d:
                    wanted = wanted & jnp.logical_not(end_of(zz))

                @pl.when(wanted)
                def _():
                    block = zz * plane + (1 - y) * CORES + c
                    arrived(block, share, h)
                    onward = which == 1 and d == 0
                    pass_on(
                        block,
                        share,
                        h,
                        has_up & (z == 0) if onward else never,
                        has_down & (z == line - 1) if onward else never,
                        never,
                    )

    def end_line(d):
        share = share_of(1)

        @pl.loop(0, pieces)
        def _(h):
            for sign in (-1, 1):
                zz = z + sign * d

                @pl.when(there(zz) & end_of(zz))
                def _():
                    block = zz * plane + (1 - y) * CORES + c
                    arrived(block, share, h)
                    pass_on(
                        block,
                        share,
                        h,
                        has_up if sign < 0 else never,
                        has_down if sign > 0 else never,
                        never,
                    )

    ends = positions(line)
    order = sorted(ends, key=lambda group: (ends[group], group))
    starts, count = {}, 0
    for group in order:
        starts[group] = count
        count += 2 if group[0] else 1
    nothing = count * slots

    def block_of(zz, other_y, other_core):
        yy = 1 - y if other_y else y
        cc = 1 - c if other_core else c
        return zz * plane + yy * CORES + cc

    def chain_links():
        for n in (4, 5, 6, 7, 8):
            loads[n].wait()
        slot = lax.broadcasted_iota(jnp.int32, rows_v.shape, 0)
        lane = lax.broadcasted_iota(jnp.int32, rows_v.shape, 1)
        wanted = jnp.where(slot < counts_v[...], rows_v[...], -2)
        candidates = [
            (starts[group] + i, group, sign)
            for group in order
            for i, sign in enumerate((-1, 1) if group[0] else (0,))
        ]
        own = slot
        found = []
        for index, (d, other_y, other_core), sign in candidates:
            zz = z + sign * d
            ok = there(zz)
            block = jnp.where(ok, block_of(zz, other_y, other_core), 0)
            own = jnp.where((lane == block) & ok, slot + index * slots, own)
            found.append((index * slots, block, ok))

        def step(k, carry):
            before, last = carry
            for first, block, ok in found:
                ok = ok & (k < counts_s[0, block])
                row = jnp.where(ok, rows_s[k, block], -1)
                key = first + k
                before = jnp.where((wanted == row) & (own > key), jnp.maximum(before, key), before)
                last = jnp.where(lane == row, jnp.maximum(last, key), last)
            return before, last

        none = jnp.full(rows_v.shape, -1, jnp.int32)
        before, last = lax.fori_loop(0, slots, step, (none, none))
        links_v[0] = jnp.where(before < 0, nothing, before)
        links_v[1] = jnp.where(last < 0, nothing, last)
        chain[nothing] = jnp.zeros(chain.shape[1:], chain.dtype)

    def links_copy():
        return local(links_v, links_s, 11)

    def multiply(group):
        d, other_y, other_core = group
        first = starts[group]

        def one(i):
            zz = z + (2 * i - 1) * d

            @pl.when(there(zz))
            def _():
                block = block_of(zz, other_y, other_core)
                if other_core:

                    @pl.loop(0, pieces)
                    def _(h):
                        for share in range(copies):
                            arrived(block, share, h)

                seat_of = first + i
                current[seat_of] = g[block].reshape(current.shape[1:])
                products = []
                for k in range(slots):
                    products.append(
                        jnp.dot(
                            tiles_v[block, k],
                            current[seat_of, cols_s[k, block]],
                            preferred_element_type=jnp.float32,
                        )
                    )
                for k in range(slots):
                    chain[seat_of * slots + k] = products[k] + chain[links_s[0, k, block]]

        if d:

            @pl.loop(0, 2)
            def _(i):
                one(i)
        else:
            one(0)

    out_width = total.shape[1]
    half, quarter = total.shape[0] // 2, total.shape[0] // 4
    first_owner, owners = (ROWS_Y, seats - 2 * ROWS_Y) if line > 2 else (0, seats)
    part = quarter // owners
    owns = (seat >= first_owner) & (seat < first_owner + owners)

    def core_copy():
        return pltpu.make_async_remote_copy(
            src_ref=terms.at[pl.ds((1 - c) * half, half)],
            dst_ref=from_core,
            send_sem=core_send.at[0],
            recv_sem=core_recv.at[0],
            device_id=near_core,
            device_id_type=MESH,
        )

    def pair_copy():
        return pltpu.make_async_remote_copy(
            src_ref=half_sum.at[pl.ds((1 - r) * quarter, quarter)],
            dst_ref=from_x,
            send_sem=pair_send.at[0],
            recv_sem=pair_recv.at[0],
            device_id=near_x,
            device_id_type=MESH,
        )

    def part_of(owner):
        return pl.multiple_of((owner - first_owner) * part, part)

    def part_copy(owner, slot):
        return pltpu.make_async_remote_copy(
            src_ref=quarter_sum.at[pl.ds(part_of(owner), part)],
            dst_ref=from_plane.at[slot],
            send_sem=plane_send.at[0, owner],
            recv_sem=plane_recv.at[0, slot],
            device_id=seat_device(owner - seat + seats)[1],
            device_id_type=MESH,
        )

    def others(first, count, act):
        @pl.loop(first, first + count)
        def _(other):
            @pl.when(other != seat)
            def _():
                act(other)

    def share_copy(other, owner):
        device = seat_device(other - seat + seats)[1]
        where = pl.ds(c * half + r * quarter + part_of(owner), part)
        return pltpu.make_async_remote_copy(
            src_ref=total.at[where],
            dst_ref=total.at[where],
            send_sem=plane_send.at[1, other],
            recv_sem=plane_recv.at[1, owner],
            device_id=device,
            device_id_type=MESH,
        )

    def pair_back(rr):
        where = pl.ds(c * half + rr * quarter, quarter)
        return pltpu.make_async_remote_copy(
            src_ref=total.at[where],
            dst_ref=total.at[where],
            send_sem=pair_send.at[1],
            recv_sem=pair_recv.at[1],
            device_id=near_x,
            device_id_type=MESH,
        )

    def core_back(cc):
        where = pl.ds(cc * half, half)
        return pltpu.make_async_remote_copy(
            src_ref=total.at[where],
            dst_ref=total.at[where],
            send_sem=core_send.at[1],
            recv_sem=core_recv.at[1],
            device_id=near_core,
            device_id_type=MESH,
        )

    def make_terms():
        loads[2].wait()
        loads[3].wait()
        for n, operand in enumerate((features_v, aggregated_v)):
            terms[n * half : (n + 1) * half, :] = lax.dot_general(
                operand[...],
                grad_v[...],
                (((0,), (0,)), ((), ())),
                preferred_element_type=jnp.float32,
            )
        core_copy().start()

    def over_cores():
        core_copy().wait_recv()
        half_sum[...] = terms[pl.ds(pl.multiple_of(c * half, half), half), :] + from_core[...]
        pair_copy().start()

    def over_pair():
        pair_copy().wait_recv()
        quarter_sum[...] = (
            half_sum[pl.ds(pl.multiple_of(r * quarter, quarter), quarter), :] + from_x[...]
        )

        others(first_owner, owners, lambda other: part_copy(other, seat).start())

    def over_plane():
        @pl.when(owns)
        def _():
            from_plane[seat] = quarter_sum[pl.ds(part_of(seat), part), :]
            others(0, seats, lambda other: part_copy(seat, other).wait_recv())
            where = pl.ds(pl.multiple_of(c * half + r * quarter + part_of(seat), part), part)
            total[where, :] = jnp.sum(from_plane[...], axis=0) * scale
            others(0, seats, lambda other: share_copy(other, seat).start())

    def back_over_pair():
        others(first_owner, owners, lambda other: share_copy(seat, other).wait_recv())
        pair_back(r).start()

    def back_over_cores():
        pair_back(1 - r).wait_recv()
        core_back(c).start()

    def self_part():
        loads[9].wait()

        @pl.loop(0, pieces)
        def _(h):
            where = pl.ds(pl.multiple_of(h * piece_rows, piece_rows), piece_rows)
            base_v[where, :] = lax.dot_general(
                grad_v[where, :],
                w_self_v[...],
                (((1,), (1,)), ((), ())),
                preferred_element_type=jnp.float32,
            )

    for h in range(pieces):
        x_copy(h).start()
        pass_on(b, r, h, has_up, has_down, always)

    last = 2 * (line - 1) + 1
    events = [
        (0.1, make_terms),
        (0.2, chain_links),
        (0.3, lambda: links_copy().start()),
        (0.9, over_cores),
        (1.0, from_across),
        (1.45, lambda: (links_copy().wait(), loads[10].wait())),
        (1.9, over_pair),
        (2.9, self_part),
        (3.9, over_plane),
        (5.9, back_over_pair),
        (6.7, back_over_cores),
    ]
    for which in range(2):
        events.append((1.1 + which, functools.partial(from_y, 0, which)))
        for d in range(1, line):
            when = 2 * (d - 1) + 1 + which
            events.append((when, functools.partial(own_line, d, which)))
            if which == 0 or d < line - 1:
                late = min(when + 3, last + (d == line - 1) * 0.8) + 0.05
                events.append((late, functools.partial(from_y, d, which)))
    for d in range(1, line):
        events.append((2 * d + 1 + (d == line - 1) * 0.8, functools.partial(end_line, d)))
    for group in order:
        events.append((ends[group], functools.partial(multiply, group)))
    for _, event in sorted(events, key=lambda pair: pair[0]):
        event()

    def back_copy():
        return pltpu.make_async_remote_copy(
            src_ref=back,
            dst_ref=got_ref,
            send_sem=back_send,
            recv_sem=back_recv,
            device_id=near_x,
            device_id_type=MESH,
        )

    for t in range(share_tiles):
        row = (1 - r) * share_tiles + t
        back[t * side : (t + 1) * side, :] = chain[links_s[1, 0, row]].astype(back.dtype)
    own_half = pl.ds(pl.multiple_of(r * width, width), width)
    for t in range(share_tiles):
        if t == 1:
            back_copy().start()
        row = r * share_tiles + t
        base_v[t * side : (t + 1) * side, own_half] += chain[links_s[1, 0, row]]
    base_copy = local(base_v, base_ref, 12)
    base_copy.start()
    core_back(1 - c).wait_recv()
    sum_copy = local(total, sum_ref, 13)
    sum_copy.start()

    core_copy().wait_send()
    pair_copy().wait_send()
    pair_back(r).wait_send()
    core_back(c).wait_send()

    others(first_owner, owners, lambda other: part_copy(other, seat).wait_send())

    @pl.when(owns)
    def _():
        others(0, seats, lambda other: share_copy(other, seat).wait_send())

    @pl.loop(0, pieces)
    def _(h):
        x_copy(h).wait_send()

        @pl.loop(0, line)
        def _(zz):
            for which in range(2):
                share = share_of(which)
                block = zz * plane + y * CORES + c
                beyond = zz * plane + (1 - y) * CORES + c
                special = end_of(zz) if which else never
                goes_up = (zz <= z) & has_up
                goes_down = (zz >= z) & has_down

                @pl.when(goes_up)
                def _():
                    send(block, share, h, 0, up).wait_send()

                @pl.when(goes_down)
                def _():
                    send(block, share, h, 1, down).wait_send()

                @pl.when(jnp.logical_not(special) | (zz == z))
                def _():
                    send(block, share, h, 2, near_y).wait_send()

                send(block, share, h, 3, near_core).wait_send()

                @pl.when(special & goes_up)
                def _():
                    send(beyond, share, h, 0, up).wait_send()

                @pl.when(special & goes_down)
                def _():
                    send(beyond, share, h, 1, down).wait_send()

                send(beyond, share, h, 3, near_core).wait_send()

    sum_copy.wait()
    base_copy.wait()
    back_copy().wait_send()
    back_copy().wait_recv()


def layer(rows, cols, counts, features, aggregated, grad, w_self, w_neigh, tiles, scale, blocks, copies):
    share_rows, width = grad.shape
    half = width // copies
    _, slots, side, _ = tiles.shape
    line = blocks // (CORES * ROWS_Y)
    seats = line * ROWS_Y
    piece_rows = share_rows // PIECES
    owners = seats - 2 * ROWS_Y if line > 2 else seats
    count = 2 * CORES * (2 * line - 1)
    bf16, f32, i32 = jnp.bfloat16, jnp.float32, jnp.int32
    dma = pltpu.SemaphoreType.DMA
    operands = (rows, cols, counts, features, aggregated, grad, w_self, w_neigh, tiles)
    return pl.pallas_call(
        functools.partial(layer_kernel, blocks, copies, scale),
        out_shape=(
            jax.ShapeDtypeStruct((share_rows, width), f32),
            jax.ShapeDtypeStruct((share_rows, half), bf16),
            jax.ShapeDtypeStruct((2 * width, width), f32),
        ),
        in_specs=[pl.BlockSpec(memory_space=pl.ANY)] * 9,
        out_specs=(pl.BlockSpec(memory_space=pl.ANY),) * 3,
        scratch_shapes=[
            pltpu.VMEM(rows.shape, i32),
            pltpu.VMEM(counts.shape, i32),
            pltpu.SMEM(rows.shape, i32),
            pltpu.SMEM(cols.shape, i32),
            pltpu.SMEM(counts.shape, i32),
            pltpu.VMEM(features.shape, bf16),
            pltpu.VMEM(aggregated.shape, bf16),
            pltpu.VMEM(grad.shape, bf16),
            pltpu.VMEM(w_self.shape, bf16),
            pltpu.VMEM(w_neigh.shape, bf16),
            pltpu.VMEM(tiles.shape, bf16),
            pltpu.VMEM((blocks, copies, PIECES, piece_rows, half), bf16),
            pltpu.VMEM((PIECES, piece_rows, half), bf16),
            pltpu.VMEM((count, copies * share_rows // side, side, half), bf16),
            pltpu.VMEM((count * slots + 1, side, half), f32),
            pltpu.VMEM((2, *rows.shape), i32),
            pltpu.SMEM((2, *rows.shape), i32),
            pltpu.VMEM((share_rows, width), f32),
            pltpu.VMEM((share_rows, half), bf16),
            pltpu.VMEM((2 * width, width), f32),
            pltpu.VMEM((width, width), f32),
            pltpu.VMEM((width, width), f32),
            pltpu.VMEM((width // 2, width), f32),
            pltpu.VMEM((width // 2, width), f32),
            pltpu.VMEM((seats, width // 2 // owners, width), f32),
            pltpu.VMEM((2 * width, width), f32),
            dma((14,)),
            dma((4, blocks, copies, PIECES)),
            dma((blocks, copies, PIECES)),
            dma((PIECES,)),
            dma,
            dma,
            dma((2,)),
            dma((2,)),
            dma((2,)),
            dma((2,)),
            dma((2, seats)),
            dma((2, seats)),
        ],
        compiler_params=pltpu.CompilerParams(collective_id=0, has_side_effects=True, vmem_limit_bytes=48 << 20),
    )(*(pltpu.with_memory_space_constraint(operand, pltpu.HBM) for operand in operands))


def by_columns(
    features, aggregated, out_grad, w_self, w_neigh, tiles, tile_rows, tile_cols, tile_counts
):
    blocks, copies = lax.axis_size("blk"), lax.axis_size("rep")
    r = lax.axis_index("rep")
    rows, width = out_grad.shape
    half = width // copies
    scale = (rows * blocks * copies) ** (-0.5)
    base, got, sums = layer(
        tile_rows[0].T,
        tile_cols[0].T,
        tile_counts,
        features,
        aggregated,
        out_grad,
        w_self,
        w_neigh,
        tiles[0],
        scale,
        blocks,
        copies,
    )
    other = (jnp.arange(width, dtype=jnp.int32) // half)[None, :] != r
    got = jnp.concatenate([got, got], axis=1).astype(jnp.float32)
    feature_grad = base + jnp.where(other, got, jnp.zeros_like(got))
    return (feature_grad, sums[:width], sums[width:])


def on_device(
    features, aggregated, out_grad, w_self, w_neigh, tiles, tile_rows, tile_cols, tile_counts
):
    block_total = lax.axis_size("blk")
    copies = lax.axis_size("rep")
    replica = lax.axis_index("rep")
    width = out_grad.shape[1]
    side = tiles.shape[-1]
    slots_total = tiles.shape[2]
    share = jnp.dot(out_grad, w_neigh.T, preferred_element_type=jnp.float32).astype(jnp.bfloat16)
    whole = lax.all_gather(share, "rep", axis=0, tiled=True)
    block_rows = whole.shape[0]
    tiles_side = block_rows // side
    pieces_whole = whole.reshape(tiles_side, side, width)
    per_copy = (slots_total + copies - 1) // copies
    slot_ids = replica + copies * jnp.arange(per_copy, dtype=jnp.int32)
    valid = slot_ids < slots_total
    safe = jnp.minimum(slot_ids, slots_total - 1)
    wanted = jnp.take(tile_cols[0], safe, axis=1)
    found = pieces_whole[lax.all_to_all(wanted, "blk", split_axis=0, concat_axis=0, tiled=True)]
    fetched = lax.all_to_all(found, "blk", split_axis=0, concat_axis=0, tiled=True)
    chosen_tiles = jnp.take(tiles[0], safe, axis=1)
    products = jnp.einsum(
        "ikpq,ikqf->ikpf", chosen_tiles, fetched, preferred_element_type=jnp.float32
    )
    live = valid[None, :] & (slot_ids[None, :] < tile_counts[0][:, None])
    products = jnp.where(live[:, :, None, None], products, jnp.zeros_like(products))
    target_rows = jnp.take(tile_rows[0], safe, axis=1).reshape(-1)
    accumulated = jnp.zeros((tiles_side, side, width), jnp.float32)
    accumulated = accumulated.at[target_rows].add(products.reshape(-1, side, width))
    flat = accumulated.reshape(block_rows, width)
    self_part = jnp.dot(out_grad, w_self.T, preferred_element_type=jnp.float32)
    contract = (((0,), (0,)), ((), ()))
    terms_self = lax.dot_general(features, out_grad, contract, preferred_element_type=jnp.float32)
    terms_neigh = lax.dot_general(
        aggregated, out_grad, contract, preferred_element_type=jnp.float32
    )
    scale = (out_grad.shape[0] * block_total * copies) ** (-0.5)
    spread_share = lax.psum_scatter(flat, "rep", scatter_dimension=0, tiled=True)
    self_sum, neigh_sum = lax.psum((terms_self, terms_neigh), ("blk", "rep"))
    return (spread_share + self_part, self_sum * scale, neigh_sum * scale)


def solution(mesh):
    blocks, copies = mesh.shape["blk"], mesh.shape["rep"]
    by_pairs = copies == 2 and blocks % (CORES * ROWS_Y) == 0
    placed = (
        P(("blk", "rep"), None),
        P(("blk", "rep"), None),
        P(("blk", "rep"), None),
        P(),
        P(),
        P("blk", None, None, None, None),
        P("blk", None, None),
        P("blk", None, None),
        P("blk", None),
    )
    return jax.shard_map(
        by_columns if by_pairs else on_device,
        mesh=mesh,
        in_specs=placed,
        out_specs=(P(("blk", "rep"), None), P(), P()),
        check_vma=False,
    )
```

```python
import functools

import jax
import jax.numpy as jnp
from jax import lax
from jax.experimental import pallas as pl
from jax.experimental.pallas import tpu as pltpu
from jax.sharding import PartitionSpec as P

MESH = pl.DeviceIdType.MESH
CORES, ROWS_Y = 2, 2


CHUNKS = 2


def schedule(line):
    last = line - 1
    own, across, ends, uses = {}, {}, {}, {}
    for h in range(CHUNKS):
        for w in range(2):
            across[0, w, h] = 1.1 + w + 0.01 * h
            own[1, w, h] = 1 + w + 0.01 * h
            across[1, w, h] = 4.05 + 0.5 * w + 0.01 * h
            for d in range(2, line):
                later = w + h if d == last else w + 1.05 * h
                own[d, w, h] = 2 * d - 1.5 + (later if w == 0 or d < last else 0.5 + 1.5 * h)
                across[d, w, h] = 2 * d + (h + 0.1 if d == last else 1.55 + 0.05 * w + (0.5 + 0.5 * w) * h)
        ends[1, h] = 3 + 0.01 * h
        for d in range(2, line):
            ends[d, h] = 2 * d + (h + 0.05 if d == last else 0.5 + 0.5 * h)
        for d in range(line):
            uses[d, 0, 0, h] = max(own[d, 1, h] if d else 1.0, 1.5) + 0.03
            uses[d, 1, 0, h] = (
                0.03
                + max(
                    [across[d, 0, h]]
                    + ([across[d, 1, h]] if d < last else [])
                    + ([ends[d, h]] if d else [])
                )
            )
            for other in range(2):
                when = uses[d, other, 0, h]
                uses[d, other, 1, h] = when + (0.45 if when < 2 * last else 0.1)
    return own, across, ends, uses


def layer_kernel(
    blocks,
    copies,
    scale,
    rows_ref,
    cols_ref,
    counts_ref,
    features_ref,
    aggregated_ref,
    grad_ref,
    w_self_ref,
    w_neigh_ref,
    tiles_ref,
    base_v,
    sum_ref,
    rows_v,
    counts_v,
    rows_s,
    cols_s,
    counts_s,
    features_v,
    aggregated_v,
    grad_v,
    w_self_v,
    w_neigh_v,
    tiles_v,
    g,
    across,
    current,
    chain,
    links_v,
    links_s,
    back,
    got,
    terms,
    from_core,
    half_sum,
    from_x,
    quarter_sum,
    from_plane,
    total,
    local_sem,
    send_sem,
    recv_sem,
    x_send,
    back_send,
    back_recv,
    core_send,
    core_recv,
    pair_send,
    pair_recv,
    plane_send,
    plane_recv,
):
    b = lax.axis_index("blk")
    r = lax.axis_index("rep")
    plane = CORES * ROWS_Y
    line = blocks // plane
    z, y, c = b // plane, (b // CORES) % ROWS_Y, b % CORES
    near_x = (b, 1 - r)
    near_core = (z * plane + y * CORES + (1 - c), r)
    near_y = (z * plane + (1 - y) * CORES + c, r)
    up, down = (b + plane, r), (b - plane, r)
    has_up, has_down = z < line - 1, z > 0
    never = z < 0
    always = z >= 0
    chunks, chunk_rows, width = g.shape[2:]
    slots, side = tiles_v.shape[1], tiles_v.shape[2]
    share_tiles = chunks * chunk_rows // side
    packed_tiles = chunk_rows // side
    of_lane = lax.broadcasted_iota(jnp.int32, (side, width), 1) // (width // chunks)
    seats = line * ROWS_Y
    seat = z * ROWS_Y + y
    end_of = lambda zz: (zz == 0) | (zz == line - 1)

    def local(src, dst, n):
        return pltpu.make_async_copy(src, dst, local_sem.at[n])

    loads = [
        local(grad_ref, grad_v, 0),
        local(w_neigh_ref, w_neigh_v, 1),
        local(features_ref, features_v, 2),
        local(aggregated_ref, aggregated_v, 3),
        local(rows_ref, rows_v, 4),
        local(counts_ref, counts_v, 5),
        local(rows_ref, rows_s, 6),
        local(cols_ref, cols_s, 7),
        local(counts_ref, counts_s, 8),
        local(w_self_ref, w_self_v, 9),
        local(tiles_ref, tiles_v, 10),
    ]
    for load in loads:
        load.start()

    barrier = pltpu.get_barrier_semaphore()

    def greet(device):
        pl.semaphore_signal(barrier, inc=1, device_id=device, device_id_type=MESH)

    def seat_device(step):
        other = (seat + step) % seats
        return other, ((other // ROWS_Y) * plane + (other % ROWS_Y) * CORES + c, r)

    greet(near_x)
    greet(near_core)

    @pl.loop(1, seats)
    def _(step):
        greet(seat_device(step)[1])

    loads[0].wait()
    loads[1].wait()

    features_each = width // chunks

    def message(which, h):
        first = pl.multiple_of(which * width + h * features_each, features_each)
        chosen = w_neigh_v[pl.ds(first, features_each), :]
        blank = jnp.zeros_like(chosen)
        packed = [
            lax.dot_general(
                grad_v[q * chunk_rows : (q + 1) * chunk_rows, :],
                jnp.concatenate([chosen if n == q else blank for n in range(chunks)], axis=0),
                (((1,), (1,)), ((), ())),
                preferred_element_type=jnp.float32,
            )
            for q in range(chunks)
        ]
        return sum(packed[1:], packed[0]).astype(g.dtype)

    for h in range(chunks):
        g[b, r, h] = message(r, h)
    for h in range(chunks):
        across[h] = message(1 - r, h)

    pl.semaphore_wait(barrier, 2 + seats - 1)

    def send(block, share, h, way, device):
        return pltpu.make_async_remote_copy(
            src_ref=g.at[block, share, h],
            dst_ref=g.at[block, share, h],
            send_sem=send_sem.at[way, block, share, h],
            recv_sem=recv_sem.at[block, share, h],
            device_id=device,
            device_id_type=MESH,
        )

    def x_copy(h):
        return pltpu.make_async_remote_copy(
            src_ref=across.at[h],
            dst_ref=g.at[b, r, h],
            send_sem=x_send.at[h],
            recv_sem=recv_sem.at[b, r, h],
            device_id=near_x,
            device_id_type=MESH,
        )

    def arrived(block, share, h):
        send(block, share, h, 3, near_core).wait_recv()

    def pass_on(block, share, h, go_up, go_down, go_y):
        @pl.when(go_up)
        def _():
            send(block, share, h, 0, up).start()

        @pl.when(go_down)
        def _():
            send(block, share, h, 1, down).start()

        @pl.when(go_y)
        def _():
            send(block, share, h, 2, near_y).start()

        send(block, share, h, 3, near_core).start()

    def share_of(which):
        return r if which == 0 else 1 - r

    def there(zz):
        return (zz >= 0) & (zz < line)

    def own_line(d, which, h):
        share = share_of(which)

        for sign in (-1, 1):
            zz = z + sign * d

            @pl.when(there(zz))
            def _():
                block = zz * plane + y * CORES + c
                arrived(block, share, h)
                pass_on(
                    block,
                    share,
                    h,
                    has_up if sign < 0 else never,
                    has_down if sign > 0 else never,
                    jnp.logical_not(end_of(zz)) if which else always,
                )

    def from_across(h):
        arrived(b, 1 - r, h)
        pass_on(b, 1 - r, h, has_up, has_down, always)

    def from_y(d, which, h):
        share = share_of(which)

        for sign in (-1, 1) if d else (0,):
            zz = z + sign * d
            wanted = there(zz)
            if which and d:
                wanted = wanted & jnp.logical_not(end_of(zz))

            @pl.when(wanted)
            def _():
                block = zz * plane + (1 - y) * CORES + c
                arrived(block, share, h)
                onward = which == 1 and d == 0
                pass_on(
                    block,
                    share,
                    h,
                    has_up & (z == 0) if onward else never,
                    has_down & (z == line - 1) if onward else never,
                    never,
                )

    def end_line(d, h):
        share = share_of(1)

        for sign in (-1, 1):
            zz = z + sign * d

            @pl.when(there(zz) & end_of(zz))
            def _():
                block = zz * plane + (1 - y) * CORES + c
                arrived(block, share, h)
                pass_on(
                    block,
                    share,
                    h,
                    has_up if sign < 0 else never,
                    has_down if sign > 0 else never,
                    never,
                )

    own_times, y_times, end_times, use_times = schedule(line)
    order = sorted(
        (group[:3] for group in use_times if group[3] == 0),
        key=lambda group: (use_times[(*group, 0)], group),
    )
    starts, count = {}, 0
    for group in order:
        starts[group] = count
        count += 2 if group[0] else 1
    nothing = count * slots

    def block_of(zz, other_y, other_core):
        yy = 1 - y if other_y else y
        cc = 1 - c if other_core else c
        return zz * plane + yy * CORES + cc

    def chain_links():
        for n in (4, 5, 6, 7, 8):
            loads[n].wait()
        slot = lax.broadcasted_iota(jnp.int32, rows_v.shape, 0)
        lane = lax.broadcasted_iota(jnp.int32, rows_v.shape, 1)
        wanted = jnp.where(slot < counts_v[...], rows_v[...], -2)
        candidates = [
            (starts[group] + i, group, sign)
            for group in order
            for i, sign in enumerate((-1, 1) if group[0] else (0,))
        ]
        own = slot
        found = []
        for index, (d, other_y, other_core), sign in candidates:
            zz = z + sign * d
            ok = there(zz)
            block = jnp.where(ok, block_of(zz, other_y, other_core), 0)
            own = jnp.where((lane == block) & ok, slot + index * slots, own)
            found.append((index * slots, block, ok))

        def step(k, carry):
            before, last = carry
            for first, block, ok in found:
                ok = ok & (k < counts_s[0, block])
                row = jnp.where(ok, rows_s[k, block], -1)
                key = first + k
                before = jnp.where((wanted == row) & (own > key), jnp.maximum(before, key), before)
                last = jnp.where(lane == row, jnp.maximum(last, key), last)
            return before, last

        none = jnp.full(rows_v.shape, -1, jnp.int32)
        before, last = lax.fori_loop(0, slots, step, (none, none))
        links_v[0] = jnp.where(before < 0, nothing, before)
        links_v[1] = jnp.where(last < 0, nothing, last)
        for h in range(chunks):
            chain[h, nothing] = jnp.zeros(chain.shape[2:], chain.dtype)

    def links_copy():
        return local(links_v, links_s, 11)

    def multiply(group, h):
        d, other_y, other_core = group
        first = starts[group]

        def one(i):
            zz = z + (2 * i - 1) * d

            @pl.when(there(zz))
            def _():
                block = block_of(zz, other_y, other_core)
                if other_core:
                    for share in range(copies):
                        arrived(block, share, h)

                seat_of = first + i
                for share in range(copies):
                    current[seat_of, share] = g[block, share, h].reshape(current.shape[2:])
                products = []
                for k in range(slots):
                    column = cols_s[k, block]
                    share, within = column // share_tiles, column % share_tiles
                    piece = current[seat_of, share, within % packed_tiles]
                    piece = jnp.where(of_lane == within // packed_tiles, piece, jnp.zeros_like(piece))
                    products.append(
                        jnp.dot(tiles_v[block, k], piece, preferred_element_type=jnp.float32)
                    )
                for k in range(slots):
                    chain[h, seat_of * slots + k] = products[k] + chain[h, links_s[0, k, block]]

        if d:

            @pl.loop(0, 2)
            def _(i):
                one(i)
        else:
            one(0)

    out_width = total.shape[1]
    half, quarter = total.shape[0] // 2, total.shape[0] // 4
    first_owner, owners = (ROWS_Y, seats - 2 * ROWS_Y) if line > 2 else (0, seats)
    part = quarter // owners
    owns = (seat >= first_owner) & (seat < first_owner + owners)

    def core_copy():
        return pltpu.make_async_remote_copy(
            src_ref=terms.at[pl.ds((1 - c) * half, half)],
            dst_ref=from_core,
            send_sem=core_send.at[0],
            recv_sem=core_recv.at[0],
            device_id=near_core,
            device_id_type=MESH,
        )

    def pair_copy():
        return pltpu.make_async_remote_copy(
            src_ref=half_sum.at[pl.ds((1 - r) * quarter, quarter)],
            dst_ref=from_x,
            send_sem=pair_send.at[0],
            recv_sem=pair_recv.at[0],
            device_id=near_x,
            device_id_type=MESH,
        )

    def part_of(owner):
        return pl.multiple_of((owner - first_owner) * part, part)

    def part_copy(owner, slot):
        return pltpu.make_async_remote_copy(
            src_ref=quarter_sum.at[pl.ds(part_of(owner), part)],
            dst_ref=from_plane.at[slot],
            send_sem=plane_send.at[0, owner],
            recv_sem=plane_recv.at[0, slot],
            device_id=seat_device(owner - seat + seats)[1],
            device_id_type=MESH,
        )

    def others(first, count, act):
        @pl.loop(first, first + count)
        def _(other):
            @pl.when(other != seat)
            def _():
                act(other)

    def share_copy(other, owner):
        device = seat_device(other - seat + seats)[1]
        where = pl.ds(c * half + r * quarter + part_of(owner), part)
        return pltpu.make_async_remote_copy(
            src_ref=total.at[where],
            dst_ref=total.at[where],
            send_sem=plane_send.at[1, other],
            recv_sem=plane_recv.at[1, owner],
            device_id=device,
            device_id_type=MESH,
        )

    def pair_back(rr):
        where = pl.ds(c * half + rr * quarter, quarter)
        return pltpu.make_async_remote_copy(
            src_ref=total.at[where],
            dst_ref=total.at[where],
            send_sem=pair_send.at[1],
            recv_sem=pair_recv.at[1],
            device_id=near_x,
            device_id_type=MESH,
        )

    def core_back(cc):
        where = pl.ds(cc * half, half)
        return pltpu.make_async_remote_copy(
            src_ref=total.at[where],
            dst_ref=total.at[where],
            send_sem=core_send.at[1],
            recv_sem=core_recv.at[1],
            device_id=near_core,
            device_id_type=MESH,
        )

    def make_terms():
        loads[2].wait()
        loads[3].wait()
        for n, operand in enumerate((features_v, aggregated_v)):
            terms[n * half : (n + 1) * half, :] = lax.dot_general(
                operand[...],
                grad_v[...],
                (((0,), (0,)), ((), ())),
                preferred_element_type=jnp.float32,
            )
        core_copy().start()

    def over_cores():
        core_copy().wait_recv()
        half_sum[...] = terms[pl.ds(pl.multiple_of(c * half, half), half), :] + from_core[...]
        pair_copy().start()

    def over_pair():
        pair_copy().wait_recv()
        quarter_sum[...] = (
            half_sum[pl.ds(pl.multiple_of(r * quarter, quarter), quarter), :] + from_x[...]
        )

        others(first_owner, owners, lambda other: part_copy(other, seat).start())

    def over_plane():
        @pl.when(owns)
        def _():
            from_plane[seat] = quarter_sum[pl.ds(part_of(seat), part), :]
            others(0, seats, lambda other: part_copy(seat, other).wait_recv())
            where = pl.ds(pl.multiple_of(c * half + r * quarter + part_of(seat), part), part)
            total[where, :] = jnp.sum(from_plane[...], axis=0) * scale
            others(0, seats, lambda other: share_copy(other, seat).start())

    def back_over_pair():
        others(first_owner, owners, lambda other: share_copy(seat, other).wait_recv())
        pair_back(r).start()

    def back_over_cores():
        pair_back(1 - r).wait_recv()
        core_back(c).start()

    def self_part():
        loads[9].wait()

        @pl.loop(0, chunks)
        def _(h):
            where = pl.ds(pl.multiple_of(h * chunk_rows, chunk_rows), chunk_rows)
            base_v[where, :] = lax.dot_general(
                grad_v[where, :],
                w_self_v[...],
                (((1,), (1,)), ((), ())),
                preferred_element_type=jnp.float32,
            )

    for h in range(chunks):
        x_copy(h).start()
        pass_on(b, r, h, has_up, has_down, always)

    def back_copy(h):
        return pltpu.make_async_remote_copy(
            src_ref=back.at[h],
            dst_ref=got.at[h],
            send_sem=back_send.at[h],
            recv_sem=back_recv.at[h],
            device_id=near_x,
            device_id_type=MESH,
        )

    own_half = pl.ds(pl.multiple_of(r * width, width), width)
    other_half = pl.ds(pl.multiple_of((1 - r) * width, width), width)

    def turned(value):
        return pltpu.roll(value, width // chunks, 1)

    def whole(h, row):
        value = chain[h, links_s[1, 0, row]]
        return value + turned(value)

    def give_back(h):
        for t in range(packed_tiles):
            row = (1 - r) * share_tiles + t
            low, high = whole(h, row), whole(h, row + packed_tiles)
            back[h, t * side : (t + 1) * side, :] = jnp.where(of_lane == 0, low, high).astype(
                back.dtype
            )

    def keep(h):
        for t in range(share_tiles):
            if t == 1:
                back_copy(h).start()
            value = whole(h, r * share_tiles + t)
            value = jnp.where(of_lane == h, value, jnp.zeros_like(value))
            base_v[t * side : (t + 1) * side, own_half] += value

    def take(h):
        back_copy(h).wait_recv()
        for t in range(packed_tiles):
            value = got[h, t * side : (t + 1) * side, :].astype(jnp.float32)
            other = turned(value)
            for q in range(chunks):
                chosen = value if q == h else other
                chosen = jnp.where(of_lane == h, chosen, jnp.zeros_like(chosen))
                first = (t + q * packed_tiles) * side
                base_v[first : first + side, other_half] += chosen

    events = [
        (0.1, make_terms),
        (0.2, chain_links),
        (0.3, lambda: links_copy().start()),
        (0.9, over_cores),
        (1.45, lambda: (links_copy().wait(), loads[10].wait())),
        (1.9, over_pair),
        (2.9, self_part),
        (3.9, over_plane),
        (5.9, back_over_pair),
        (6.65, back_over_cores),
    ]
    for h in range(chunks):
        events.append((1.0 + 0.01 * h, functools.partial(from_across, h)))
    for act, times in ((own_line, own_times), (from_y, y_times), (end_line, end_times)):
        for key, when in times.items():
            if act is not from_y or key[:2] != (line - 1, 1):
                events.append((when, functools.partial(act, *key)))
    for h in range(chunks):
        when = 0
        for group in order:
            when = max(when, use_times[(*group, h)])
            events.append((when, functools.partial(multiply, group, h)))
        events.append((when + 0.001, functools.partial(give_back, h)))
        events.append((when + 0.002, functools.partial(keep, h)))
    for _, event in sorted(events, key=lambda pair: pair[0]):
        event()

    for h in range(chunks - 1):
        take(h)
    core_back(1 - c).wait_recv()
    sum_copy = local(total, sum_ref, 12)
    sum_copy.start()

    core_copy().wait_send()
    pair_copy().wait_send()
    pair_back(r).wait_send()
    core_back(c).wait_send()

    others(first_owner, owners, lambda other: part_copy(other, seat).wait_send())

    @pl.when(owns)
    def _():
        others(0, seats, lambda other: share_copy(other, seat).wait_send())

    @pl.loop(0, chunks)
    def _(h):
        x_copy(h).wait_send()

        @pl.loop(0, line)
        def _(zz):
            for which in range(2):
                share = share_of(which)
                block = zz * plane + y * CORES + c
                beyond = zz * plane + (1 - y) * CORES + c
                special = end_of(zz) if which else never
                goes_up = (zz <= z) & has_up
                goes_down = (zz >= z) & has_down

                @pl.when(goes_up)
                def _():
                    send(block, share, h, 0, up).wait_send()

                @pl.when(goes_down)
                def _():
                    send(block, share, h, 1, down).wait_send()

                @pl.when(jnp.logical_not(special) | (zz == z))
                def _():
                    send(block, share, h, 2, near_y).wait_send()

                send(block, share, h, 3, near_core).wait_send()

                @pl.when(special & goes_up)
                def _():
                    send(beyond, share, h, 0, up).wait_send()

                @pl.when(special & goes_down)
                def _():
                    send(beyond, share, h, 1, down).wait_send()

                send(beyond, share, h, 3, near_core).wait_send()

    sum_copy.wait()
    for h in range(chunks):
        back_copy(h).wait_send()
    take(chunks - 1)


def layer(rows, cols, counts, features, aggregated, grad, w_self, w_neigh, tiles, scale, blocks, copies):
    share_rows, width = grad.shape
    half = width // copies
    _, slots, side, _ = tiles.shape
    line = blocks // (CORES * ROWS_Y)
    seats = line * ROWS_Y
    chunk_rows = share_rows // CHUNKS
    owners = seats - 2 * ROWS_Y if line > 2 else seats
    count = 2 * CORES * (2 * line - 1)
    bf16, f32, i32 = jnp.bfloat16, jnp.float32, jnp.int32
    dma = pltpu.SemaphoreType.DMA
    operands = (rows, cols, counts, features, aggregated, grad, w_self, w_neigh, tiles)
    return pl.pallas_call(
        functools.partial(layer_kernel, blocks, copies, scale),
        out_shape=(
            pltpu.VMEM((share_rows, width), f32),
            pltpu.VMEM((2 * width, width), f32),
        ),
        in_specs=[pl.BlockSpec(memory_space=pl.ANY)] * 9,
        out_specs=(
            pl.BlockSpec(memory_space=pltpu.VMEM),
            pl.BlockSpec(memory_space=pl.ANY),
        ),
        scratch_shapes=[
            pltpu.VMEM(rows.shape, i32),
            pltpu.VMEM(counts.shape, i32),
            pltpu.SMEM(rows.shape, i32),
            pltpu.SMEM(cols.shape, i32),
            pltpu.SMEM(counts.shape, i32),
            pltpu.VMEM(features.shape, bf16),
            pltpu.VMEM(aggregated.shape, bf16),
            pltpu.VMEM(grad.shape, bf16),
            pltpu.VMEM(w_self.shape, bf16),
            pltpu.VMEM(w_neigh.shape, bf16),
            pltpu.VMEM(tiles.shape, bf16),
            pltpu.VMEM((blocks, copies, CHUNKS, chunk_rows, half), bf16),
            pltpu.VMEM((CHUNKS, chunk_rows, half), bf16),
            pltpu.VMEM((count, copies, chunk_rows // side, side, half), bf16),
            pltpu.VMEM((CHUNKS, count * slots + 1, side, half), f32),
            pltpu.VMEM((2, *rows.shape), i32),
            pltpu.SMEM((2, *rows.shape), i32),
            pltpu.VMEM((CHUNKS, chunk_rows, half), bf16),
            pltpu.VMEM((CHUNKS, chunk_rows, half), bf16),
            pltpu.VMEM((2 * width, width), f32),
            pltpu.VMEM((width, width), f32),
            pltpu.VMEM((width, width), f32),
            pltpu.VMEM((width // 2, width), f32),
            pltpu.VMEM((width // 2, width), f32),
            pltpu.VMEM((seats, width // 2 // owners, width), f32),
            pltpu.VMEM((2 * width, width), f32),
            dma((13,)),
            dma((4, blocks, copies, CHUNKS)),
            dma((blocks, copies, CHUNKS)),
            dma((CHUNKS,)),
            dma((CHUNKS,)),
            dma((CHUNKS,)),
            dma((2,)),
            dma((2,)),
            dma((2,)),
            dma((2,)),
            dma((2, seats)),
            dma((2, seats)),
        ],
        compiler_params=pltpu.CompilerParams(collective_id=0, has_side_effects=True, vmem_limit_bytes=54 << 20),
    )(*(pltpu.with_memory_space_constraint(operand, pltpu.HBM) for operand in operands))


def by_columns(
    features, aggregated, out_grad, w_self, w_neigh, tiles, tile_rows, tile_cols, tile_counts
):
    blocks, copies = lax.axis_size("blk"), lax.axis_size("rep")
    rows, width = out_grad.shape
    scale = (rows * blocks * copies) ** (-0.5)
    feature_grad, sums = layer(
        tile_rows[0].T,
        tile_cols[0].T,
        tile_counts,
        features,
        aggregated,
        out_grad,
        w_self,
        w_neigh,
        tiles[0],
        scale,
        blocks,
        copies,
    )
    return (feature_grad, sums[:width], sums[width:])


def on_device(
    features, aggregated, out_grad, w_self, w_neigh, tiles, tile_rows, tile_cols, tile_counts
):
    block_total = lax.axis_size("blk")
    copies = lax.axis_size("rep")
    replica = lax.axis_index("rep")
    width = out_grad.shape[1]
    side = tiles.shape[-1]
    slots_total = tiles.shape[2]
    share = jnp.dot(out_grad, w_neigh.T, preferred_element_type=jnp.float32).astype(jnp.bfloat16)
    whole = lax.all_gather(share, "rep", axis=0, tiled=True)
    block_rows = whole.shape[0]
    tiles_side = block_rows // side
    chunks_whole = whole.reshape(tiles_side, side, width)
    per_copy = (slots_total + copies - 1) // copies
    slot_ids = replica + copies * jnp.arange(per_copy, dtype=jnp.int32)
    valid = slot_ids < slots_total
    safe = jnp.minimum(slot_ids, slots_total - 1)
    wanted = jnp.take(tile_cols[0], safe, axis=1)
    found = chunks_whole[lax.all_to_all(wanted, "blk", split_axis=0, concat_axis=0, tiled=True)]
    fetched = lax.all_to_all(found, "blk", split_axis=0, concat_axis=0, tiled=True)
    chosen_tiles = jnp.take(tiles[0], safe, axis=1)
    products = jnp.einsum(
        "ikpq,ikqf->ikpf", chosen_tiles, fetched, preferred_element_type=jnp.float32
    )
    live = valid[None, :] & (slot_ids[None, :] < tile_counts[0][:, None])
    products = jnp.where(live[:, :, None, None], products, jnp.zeros_like(products))
    target_rows = jnp.take(tile_rows[0], safe, axis=1).reshape(-1)
    accumulated = jnp.zeros((tiles_side, side, width), jnp.float32)
    accumulated = accumulated.at[target_rows].add(products.reshape(-1, side, width))
    flat = accumulated.reshape(block_rows, width)
    self_part = jnp.dot(out_grad, w_self.T, preferred_element_type=jnp.float32)
    contract = (((0,), (0,)), ((), ()))
    terms_self = lax.dot_general(features, out_grad, contract, preferred_element_type=jnp.float32)
    terms_neigh = lax.dot_general(
        aggregated, out_grad, contract, preferred_element_type=jnp.float32
    )
    scale = (out_grad.shape[0] * block_total * copies) ** (-0.5)
    spread_share = lax.psum_scatter(flat, "rep", scatter_dimension=0, tiled=True)
    self_sum, neigh_sum = lax.psum((terms_self, terms_neigh), ("blk", "rep"))
    return (spread_share + self_part, self_sum * scale, neigh_sum * scale)


def solution(mesh):
    blocks, copies = mesh.shape["blk"], mesh.shape["rep"]
    by_pairs = copies == 2 and blocks % (CORES * ROWS_Y) == 0 and blocks > 2 * CORES * ROWS_Y
    placed = (
        P(("blk", "rep"), None),
        P(("blk", "rep"), None),
        P(("blk", "rep"), None),
        P(),
        P(),
        P("blk", None, None, None, None),
        P("blk", None, None),
        P("blk", None, None),
        P("blk", None),
    )
    return jax.shard_map(
        by_columns if by_pairs else on_device,
        mesh=mesh,
        in_specs=placed,
        out_specs=(P(("blk", "rep"), None), P(), P()),
        check_vma=False,
    )
```

```python
import functools

import jax
import jax.numpy as jnp
from jax import lax
from jax.experimental import pallas as pl
from jax.experimental.pallas import tpu as pltpu
from jax.sharding import PartitionSpec as P

MESH = pl.DeviceIdType.MESH
CORES, ROWS_Y = 2, 2


CHUNKS = 2


def schedule(line):
    last = line - 1
    own, across, ends, uses = {}, {}, {}, {}
    for h in range(CHUNKS):
        for w in range(2):
            across[0, w, h] = 1.1 + w + 0.01 * h
            own[1, w, h] = 1 + w + 0.01 * h
            across[1, w, h] = 4.05 + 0.5 * w + 0.01 * h
            for d in range(2, line):
                later = w + h if d == last else w + 1.05 * h
                own[d, w, h] = 2 * d - 1.5 + (later if w == 0 or d < last else 0.5 + 1.5 * h)
                across[d, w, h] = 2 * d + (h + 0.1 if d == last else 1.55 + 0.05 * w + (0.5 + 0.5 * w) * h)
        ends[1, h] = 3 + 0.01 * h
        for d in range(2, line):
            ends[d, h] = 2 * d + (h + 0.05 if d == last else 0.5 + 0.5 * h)
        for d in range(line):
            uses[d, 0, 0, h] = max(own[d, 1, h] if d else 1.0, 1.5) + 0.03
            uses[d, 1, 0, h] = (
                0.03
                + max(
                    [across[d, 0, h]]
                    + ([across[d, 1, h]] if d < last else [])
                    + ([ends[d, h]] if d else [])
                )
            )
            for other in range(2):
                when = uses[d, other, 0, h]
                uses[d, other, 1, h] = when + (0.45 if when < 2 * last else 0.1)
    return own, across, ends, uses


def layer_kernel(
    blocks,
    copies,
    scale,
    rows_ref,
    cols_ref,
    counts_ref,
    features_ref,
    aggregated_ref,
    grad_ref,
    w_self_ref,
    w_neigh_ref,
    tiles_ref,
    base_v,
    total,
    rows_v,
    counts_v,
    rows_s,
    cols_s,
    counts_s,
    features_v,
    aggregated_v,
    grad_v,
    w_self_v,
    w_neigh_v,
    tiles_v,
    g,
    across,
    current,
    chain,
    links_v,
    links_s,
    back,
    got,
    terms,
    from_core,
    half_sum,
    from_x,
    quarter_sum,
    from_plane,
    local_sem,
    send_sem,
    recv_sem,
    x_send,
    back_send,
    back_recv,
    core_send,
    core_recv,
    pair_send,
    pair_recv,
    plane_send,
    plane_recv,
):
    b = lax.axis_index("blk")
    r = lax.axis_index("rep")
    plane = CORES * ROWS_Y
    line = blocks // plane
    z, y, c = b // plane, (b // CORES) % ROWS_Y, b % CORES
    near_x = (b, 1 - r)
    near_core = (z * plane + y * CORES + (1 - c), r)
    near_y = (z * plane + (1 - y) * CORES + c, r)
    up, down = (b + plane, r), (b - plane, r)
    has_up, has_down = z < line - 1, z > 0
    never = z < 0
    always = z >= 0
    chunks, chunk_rows, width = g.shape[2:]
    slots, side = tiles_v.shape[1], tiles_v.shape[2]
    share_tiles = chunks * chunk_rows // side
    packed_tiles = chunk_rows // side
    of_lane = lax.broadcasted_iota(jnp.int32, (side, width), 1) // (width // chunks)
    seats = line * ROWS_Y
    seat = z * ROWS_Y + y
    end_of = lambda zz: (zz == 0) | (zz == line - 1)

    def local(src, dst, n):
        return pltpu.make_async_copy(src, dst, local_sem.at[n])

    loads = [
        local(grad_ref, grad_v, 0),
        local(w_neigh_ref, w_neigh_v, 1),
        local(features_ref, features_v, 2),
        local(aggregated_ref, aggregated_v, 3),
        local(rows_ref, rows_v, 4),
        local(counts_ref, counts_v, 5),
        local(rows_ref, rows_s, 6),
        local(cols_ref, cols_s, 7),
        local(counts_ref, counts_s, 8),
        local(w_self_ref, w_self_v, 9),
        local(tiles_ref, tiles_v, 10),
    ]
    for load in loads:
        load.start()

    barrier = pltpu.get_barrier_semaphore()

    def greet(device):
        pl.semaphore_signal(barrier, inc=1, device_id=device, device_id_type=MESH)

    def seat_device(step):
        other = (seat + step) % seats
        return other, ((other // ROWS_Y) * plane + (other % ROWS_Y) * CORES + c, r)

    greet(near_x)
    greet(near_core)

    @pl.loop(1, seats)
    def _(step):
        greet(seat_device(step)[1])

    loads[0].wait()
    loads[1].wait()

    features_each = width // chunks

    def message(which, h):
        first = pl.multiple_of(which * width + h * features_each, features_each)
        chosen = w_neigh_v[pl.ds(first, features_each), :]
        blank = jnp.zeros_like(chosen)
        packed = [
            lax.dot_general(
                grad_v[q * chunk_rows : (q + 1) * chunk_rows, :],
                jnp.concatenate([chosen if n == q else blank for n in range(chunks)], axis=0),
                (((1,), (1,)), ((), ())),
                preferred_element_type=jnp.float32,
            )
            for q in range(chunks)
        ]
        return sum(packed[1:], packed[0]).astype(g.dtype)

    for h in range(chunks):
        g[b, r, h] = message(r, h)
    for h in range(chunks):
        across[h] = message(1 - r, h)

    pl.semaphore_wait(barrier, 2 + seats - 1)

    def send(block, share, h, way, device):
        return pltpu.make_async_remote_copy(
            src_ref=g.at[block, share, h],
            dst_ref=g.at[block, share, h],
            send_sem=send_sem.at[way, block, share, h],
            recv_sem=recv_sem.at[block, share, h],
            device_id=device,
            device_id_type=MESH,
        )

    def x_copy(h):
        return pltpu.make_async_remote_copy(
            src_ref=across.at[h],
            dst_ref=g.at[b, r, h],
            send_sem=x_send.at[h],
            recv_sem=recv_sem.at[b, r, h],
            device_id=near_x,
            device_id_type=MESH,
        )

    def arrived(block, share, h):
        send(block, share, h, 3, near_core).wait_recv()

    def pass_on(block, share, h, go_up, go_down, go_y):
        @pl.when(go_up)
        def _():
            send(block, share, h, 0, up).start()

        @pl.when(go_down)
        def _():
            send(block, share, h, 1, down).start()

        @pl.when(go_y)
        def _():
            send(block, share, h, 2, near_y).start()

        send(block, share, h, 3, near_core).start()

    def share_of(which):
        return r if which == 0 else 1 - r

    def there(zz):
        return (zz >= 0) & (zz < line)

    def own_line(d, which, h):
        share = share_of(which)

        for sign in (-1, 1):
            zz = z + sign * d

            @pl.when(there(zz))
            def _():
                block = zz * plane + y * CORES + c
                arrived(block, share, h)
                pass_on(
                    block,
                    share,
                    h,
                    has_up if sign < 0 else never,
                    has_down if sign > 0 else never,
                    jnp.logical_not(end_of(zz)) if which else always,
                )

    def from_across(h):
        arrived(b, 1 - r, h)
        pass_on(b, 1 - r, h, has_up, has_down, always)

    def from_y(d, which, h):
        share = share_of(which)

        for sign in (-1, 1) if d else (0,):
            zz = z + sign * d
            wanted = there(zz)
            if which and d:
                wanted = wanted & jnp.logical_not(end_of(zz))

            @pl.when(wanted)
            def _():
                block = zz * plane + (1 - y) * CORES + c
                arrived(block, share, h)
                onward = which == 1 and d == 0
                pass_on(
                    block,
                    share,
                    h,
                    has_up & (z == 0) if onward else never,
                    has_down & (z == line - 1) if onward else never,
                    never,
                )

    def end_line(d, h):
        share = share_of(1)

        for sign in (-1, 1):
            zz = z + sign * d

            @pl.when(there(zz) & end_of(zz))
            def _():
                block = zz * plane + (1 - y) * CORES + c
                arrived(block, share, h)
                pass_on(
                    block,
                    share,
                    h,
                    has_up if sign < 0 else never,
                    has_down if sign > 0 else never,
                    never,
                )

    own_times, y_times, end_times, use_times = schedule(line)
    order = sorted(
        (group[:3] for group in use_times if group[3] == 0),
        key=lambda group: (use_times[(*group, 0)], group),
    )
    starts, count = {}, 0
    for group in order:
        starts[group] = count
        count += 2 if group[0] else 1
    nothing = count * slots

    def block_of(zz, other_y, other_core):
        yy = 1 - y if other_y else y
        cc = 1 - c if other_core else c
        return zz * plane + yy * CORES + cc

    def chain_links():
        for n in (4, 5, 6, 7, 8):
            loads[n].wait()
        slot = lax.broadcasted_iota(jnp.int32, rows_v.shape, 0)
        lane = lax.broadcasted_iota(jnp.int32, rows_v.shape, 1)
        wanted = jnp.where(slot < counts_v[...], rows_v[...], -2)
        candidates = [
            (starts[group] + i, group, sign)
            for group in order
            for i, sign in enumerate((-1, 1) if group[0] else (0,))
        ]
        own = slot
        found = []
        for index, (d, other_y, other_core), sign in candidates:
            zz = z + sign * d
            ok = there(zz)
            block = jnp.where(ok, block_of(zz, other_y, other_core), 0)
            own = jnp.where((lane == block) & ok, slot + index * slots, own)
            found.append((index * slots, block, ok))

        def step(k, carry):
            before, last = carry
            for first, block, ok in found:
                ok = ok & (k < counts_s[0, block])
                row = jnp.where(ok, rows_s[k, block], -1)
                key = first + k
                before = jnp.where((wanted == row) & (own > key), jnp.maximum(before, key), before)
                last = jnp.where(lane == row, jnp.maximum(last, key), last)
            return before, last

        none = jnp.full(rows_v.shape, -1, jnp.int32)
        before, last = lax.fori_loop(0, slots, step, (none, none))
        links_v[0] = jnp.where(before < 0, nothing, before)
        links_v[1] = jnp.where(last < 0, nothing, last)
        for h in range(chunks):
            chain[h, nothing] = jnp.zeros(chain.shape[2:], chain.dtype)

    def links_copy():
        return local(links_v, links_s, 11)

    def multiply(group, h):
        d, other_y, other_core = group
        first = starts[group]

        def one(i):
            zz = z + (2 * i - 1) * d

            @pl.when(there(zz))
            def _():
                block = block_of(zz, other_y, other_core)
                if other_core:
                    for share in range(copies):
                        arrived(block, share, h)

                seat_of = first + i
                for share in range(copies):
                    current[h, seat_of, share] = g[block, share, h].reshape(current.shape[3:])
                products = []
                for k in range(slots):
                    column = cols_s[k, block]
                    share, within = column // share_tiles, column % share_tiles
                    piece = current[h, seat_of, share, within % packed_tiles]
                    piece = jnp.where(of_lane == within // packed_tiles, piece, jnp.zeros_like(piece))
                    products.append(
                        jnp.dot(tiles_v[block, k], piece, preferred_element_type=jnp.float32)
                    )
                for k in range(slots):
                    chain[h, seat_of * slots + k] = products[k] + chain[h, links_s[0, k, block]]

        if d:

            @pl.loop(0, 2)
            def _(i):
                one(i)
        else:
            one(0)

    out_width = total.shape[1]
    half, quarter = total.shape[0] // 2, total.shape[0] // 4
    first_owner, owners = (ROWS_Y, seats - 2 * ROWS_Y) if line > 2 else (0, seats)
    part = quarter // owners
    owns = (seat >= first_owner) & (seat < first_owner + owners)

    def core_copy():
        return pltpu.make_async_remote_copy(
            src_ref=terms.at[pl.ds((1 - c) * half, half)],
            dst_ref=from_core,
            send_sem=core_send.at[0],
            recv_sem=core_recv.at[0],
            device_id=near_core,
            device_id_type=MESH,
        )

    def pair_copy():
        return pltpu.make_async_remote_copy(
            src_ref=half_sum.at[pl.ds((1 - r) * quarter, quarter)],
            dst_ref=from_x,
            send_sem=pair_send.at[0],
            recv_sem=pair_recv.at[0],
            device_id=near_x,
            device_id_type=MESH,
        )

    def part_of(owner):
        return pl.multiple_of((owner - first_owner) * part, part)

    def part_copy(owner, slot):
        return pltpu.make_async_remote_copy(
            src_ref=quarter_sum.at[pl.ds(part_of(owner), part)],
            dst_ref=from_plane.at[slot],
            send_sem=plane_send.at[0, owner],
            recv_sem=plane_recv.at[0, slot],
            device_id=seat_device(owner - seat + seats)[1],
            device_id_type=MESH,
        )

    def others(first, count, act):
        @pl.loop(first, first + count)
        def _(other):
            @pl.when(other != seat)
            def _():
                act(other)

    def share_copy(other, owner):
        device = seat_device(other - seat + seats)[1]
        where = pl.ds(c * half + r * quarter + part_of(owner), part)
        return pltpu.make_async_remote_copy(
            src_ref=total.at[where],
            dst_ref=total.at[where],
            send_sem=plane_send.at[1, other],
            recv_sem=plane_recv.at[1, owner],
            device_id=device,
            device_id_type=MESH,
        )

    def pair_back(rr):
        where = pl.ds(c * half + rr * quarter, quarter)
        return pltpu.make_async_remote_copy(
            src_ref=total.at[where],
            dst_ref=total.at[where],
            send_sem=pair_send.at[1],
            recv_sem=pair_recv.at[1],
            device_id=near_x,
            device_id_type=MESH,
        )

    def core_back(cc):
        where = pl.ds(cc * half, half)
        return pltpu.make_async_remote_copy(
            src_ref=total.at[where],
            dst_ref=total.at[where],
            send_sem=core_send.at[1],
            recv_sem=core_recv.at[1],
            device_id=near_core,
            device_id_type=MESH,
        )

    def make_terms():
        loads[2].wait()
        loads[3].wait()
        for n, operand in enumerate((features_v, aggregated_v)):
            terms[n * half : (n + 1) * half, :] = lax.dot_general(
                operand[...],
                grad_v[...],
                (((0,), (0,)), ((), ())),
                preferred_element_type=jnp.float32,
            )
        core_copy().start()

    def over_cores():
        core_copy().wait_recv()
        half_sum[...] = terms[pl.ds(pl.multiple_of(c * half, half), half), :] + from_core[...]
        pair_copy().start()

    def over_pair():
        pair_copy().wait_recv()
        quarter_sum[...] = (
            half_sum[pl.ds(pl.multiple_of(r * quarter, quarter), quarter), :] + from_x[...]
        )

        others(first_owner, owners, lambda other: part_copy(other, seat).start())

    def over_plane():
        @pl.when(owns)
        def _():
            from_plane[seat] = quarter_sum[pl.ds(part_of(seat), part), :]
            others(0, seats, lambda other: part_copy(seat, other).wait_recv())
            where = pl.ds(pl.multiple_of(c * half + r * quarter + part_of(seat), part), part)
            total[where, :] = jnp.sum(from_plane[...], axis=0) * scale
            others(0, seats, lambda other: share_copy(other, seat).start())

    def back_over_pair():
        others(first_owner, owners, lambda other: share_copy(seat, other).wait_recv())
        pair_back(r).start()

    def back_over_cores():
        pair_back(1 - r).wait_recv()
        core_back(c).start()

    def self_part():
        loads[9].wait()

        @pl.loop(0, chunks)
        def _(h):
            where = pl.ds(pl.multiple_of(h * chunk_rows, chunk_rows), chunk_rows)
            base_v[where, :] = lax.dot_general(
                grad_v[where, :],
                w_self_v[...],
                (((1,), (1,)), ((), ())),
                preferred_element_type=jnp.float32,
            )

    for h in range(chunks):
        x_copy(h).start()
        pass_on(b, r, h, has_up, has_down, always)

    def back_copy(h):
        return pltpu.make_async_remote_copy(
            src_ref=back.at[h],
            dst_ref=got.at[h],
            send_sem=back_send.at[h],
            recv_sem=back_recv.at[h],
            device_id=near_x,
            device_id_type=MESH,
        )

    own_half = pl.ds(pl.multiple_of(r * width, width), width)
    other_half = pl.ds(pl.multiple_of((1 - r) * width, width), width)

    def turned(value):
        return pltpu.roll(value, width // chunks, 1)

    def whole(h, row):
        value = chain[h, links_s[1, 0, row]]
        return value + turned(value)

    def give_back(h):
        for t in range(packed_tiles):
            row = (1 - r) * share_tiles + t
            low, high = whole(h, row), whole(h, row + packed_tiles)
            back[h, t * side : (t + 1) * side, :] = jnp.where(of_lane == 0, low, high).astype(
                back.dtype
            )

    def keep(h):
        for t in range(share_tiles):
            if t == 1:
                back_copy(h).start()
            value = whole(h, r * share_tiles + t)
            value = jnp.where(of_lane == h, value, jnp.zeros_like(value))
            base_v[t * side : (t + 1) * side, own_half] += value

    def take(h):
        back_copy(h).wait_recv()
        for t in range(packed_tiles):
            value = got[h, t * side : (t + 1) * side, :].astype(jnp.float32)
            other = turned(value)
            for q in range(chunks):
                chosen = value if q == h else other
                chosen = jnp.where(of_lane == h, chosen, jnp.zeros_like(chosen))
                first = (t + q * packed_tiles) * side
                base_v[first : first + side, other_half] += chosen

    events = [
        (0.1, make_terms),
        (0.2, chain_links),
        (0.3, lambda: links_copy().start()),
        (0.9, over_cores),
        (1.45, lambda: (links_copy().wait(), loads[10].wait())),
        (1.9, over_pair),
        (2.9, self_part),
        (3.9, over_plane),
        (5.9, back_over_pair),
        (6.65, back_over_cores),
    ]
    for h in range(chunks):
        events.append((1.0 + 0.01 * h, functools.partial(from_across, h)))
    for act, times in ((own_line, own_times), (from_y, y_times), (end_line, end_times)):
        for key, when in times.items():
            if act is not from_y or key[:2] != (line - 1, 1):
                events.append((when, functools.partial(act, *key)))
    for h in range(chunks):
        when = 0
        for group in order:
            when = max(when, use_times[(*group, h)])
            events.append((when, functools.partial(multiply, group, h)))
        events.append((when + 0.001, functools.partial(give_back, h)))
        events.append((when + 0.002, functools.partial(keep, h)))
    for _, event in sorted(events, key=lambda pair: pair[0]):
        event()

    for h in range(chunks - 1):
        take(h)
    core_back(1 - c).wait_recv()

    core_copy().wait_send()
    pair_copy().wait_send()
    pair_back(r).wait_send()
    core_back(c).wait_send()

    others(first_owner, owners, lambda other: part_copy(other, seat).wait_send())

    @pl.when(owns)
    def _():
        others(0, seats, lambda other: share_copy(other, seat).wait_send())

    @pl.loop(0, chunks)
    def _(h):
        x_copy(h).wait_send()

        @pl.loop(0, line)
        def _(zz):
            for which in range(2):
                share = share_of(which)
                block = zz * plane + y * CORES + c
                beyond = zz * plane + (1 - y) * CORES + c
                special = end_of(zz) if which else never
                goes_up = (zz <= z) & has_up
                goes_down = (zz >= z) & has_down

                @pl.when(goes_up)
                def _():
                    send(block, share, h, 0, up).wait_send()

                @pl.when(goes_down)
                def _():
                    send(block, share, h, 1, down).wait_send()

                @pl.when(jnp.logical_not(special) | (zz == z))
                def _():
                    send(block, share, h, 2, near_y).wait_send()

                send(block, share, h, 3, near_core).wait_send()

                @pl.when(special & goes_up)
                def _():
                    send(beyond, share, h, 0, up).wait_send()

                @pl.when(special & goes_down)
                def _():
                    send(beyond, share, h, 1, down).wait_send()

                send(beyond, share, h, 3, near_core).wait_send()

    for h in range(chunks):
        back_copy(h).wait_send()
    take(chunks - 1)


def layer(rows, cols, counts, features, aggregated, grad, w_self, w_neigh, tiles, scale, blocks, copies):
    share_rows, width = grad.shape
    half = width // copies
    _, slots, side, _ = tiles.shape
    line = blocks // (CORES * ROWS_Y)
    seats = line * ROWS_Y
    chunk_rows = share_rows // CHUNKS
    owners = seats - 2 * ROWS_Y if line > 2 else seats
    count = 2 * CORES * (2 * line - 1)
    bf16, f32, i32 = jnp.bfloat16, jnp.float32, jnp.int32
    dma = pltpu.SemaphoreType.DMA
    operands = (rows, cols, counts, features, aggregated, grad, w_self, w_neigh, tiles)
    return pl.pallas_call(
        functools.partial(layer_kernel, blocks, copies, scale),
        out_shape=(
            pltpu.VMEM((share_rows, width), f32),
            pltpu.VMEM((2 * width, width), f32),
        ),
        in_specs=[pl.BlockSpec(memory_space=pl.ANY)] * 9,
        out_specs=(
            pl.BlockSpec(memory_space=pltpu.VMEM),
            pl.BlockSpec(memory_space=pltpu.VMEM),
        ),
        scratch_shapes=[
            pltpu.VMEM(rows.shape, i32),
            pltpu.VMEM(counts.shape, i32),
            pltpu.SMEM(rows.shape, i32),
            pltpu.SMEM(cols.shape, i32),
            pltpu.SMEM(counts.shape, i32),
            pltpu.VMEM(features.shape, bf16),
            pltpu.VMEM(aggregated.shape, bf16),
            pltpu.VMEM(grad.shape, bf16),
            pltpu.VMEM(w_self.shape, bf16),
            pltpu.VMEM(w_neigh.shape, bf16),
            pltpu.VMEM(tiles.shape, bf16),
            pltpu.VMEM((blocks, copies, CHUNKS, chunk_rows, half), bf16),
            pltpu.VMEM((CHUNKS, chunk_rows, half), bf16),
            pltpu.VMEM((CHUNKS, count, copies, chunk_rows // side, side, half), bf16),
            pltpu.VMEM((CHUNKS, count * slots + 1, side, half), f32),
            pltpu.VMEM((2, *rows.shape), i32),
            pltpu.SMEM((2, *rows.shape), i32),
            pltpu.VMEM((CHUNKS, chunk_rows, half), bf16),
            pltpu.VMEM((CHUNKS, chunk_rows, half), bf16),
            pltpu.VMEM((2 * width, width), f32),
            pltpu.VMEM((width, width), f32),
            pltpu.VMEM((width, width), f32),
            pltpu.VMEM((width // 2, width), f32),
            pltpu.VMEM((width // 2, width), f32),
            pltpu.VMEM((seats, width // 2 // owners, width), f32),
            dma((12,)),
            dma((4, blocks, copies, CHUNKS)),
            dma((blocks, copies, CHUNKS)),
            dma((CHUNKS,)),
            dma((CHUNKS,)),
            dma((CHUNKS,)),
            dma((2,)),
            dma((2,)),
            dma((2,)),
            dma((2,)),
            dma((2, seats)),
            dma((2, seats)),
        ],
        compiler_params=pltpu.CompilerParams(collective_id=0, has_side_effects=True, vmem_limit_bytes=60 << 20),
    )(*(pltpu.with_memory_space_constraint(operand, pltpu.HBM) for operand in operands))


def finish_kernel(grad_ref, sums_ref, *refs):
    outs, sem = refs[:3], refs[3]
    width = sums_ref.shape[1]
    sources = (grad_ref, sums_ref.at[pl.ds(0, width)], sums_ref.at[pl.ds(width, width)])
    copies = [
        pltpu.make_async_copy(src, dst, sem.at[n]) for n, (src, dst) in enumerate(zip(sources, outs))
    ]
    for copy in copies:
        copy.start()
    for copy in copies:
        copy.wait()


def finish(feature_grad, sums):
    width = sums.shape[1]
    square = jax.ShapeDtypeStruct((width, width), sums.dtype)
    return pl.pallas_call(
        finish_kernel,
        out_shape=(jax.ShapeDtypeStruct(feature_grad.shape, feature_grad.dtype), square, square),
        in_specs=[pl.BlockSpec(memory_space=pl.ANY)] * 2,
        out_specs=(pl.BlockSpec(memory_space=pl.ANY),) * 3,
        scratch_shapes=[pltpu.SemaphoreType.DMA((3,))],
        compiler_params=pltpu.CompilerParams(vmem_limit_bytes=1 << 20),
    )(feature_grad, sums)


def by_columns(
    features, aggregated, out_grad, w_self, w_neigh, tiles, tile_rows, tile_cols, tile_counts
):
    blocks, copies = lax.axis_size("blk"), lax.axis_size("rep")
    rows, width = out_grad.shape
    scale = (rows * blocks * copies) ** (-0.5)
    feature_grad, sums = layer(
        tile_rows[0].T,
        tile_cols[0].T,
        tile_counts,
        features,
        aggregated,
        out_grad,
        w_self,
        w_neigh,
        tiles[0],
        scale,
        blocks,
        copies,
    )
    return finish(feature_grad, sums)


def on_device(
    features, aggregated, out_grad, w_self, w_neigh, tiles, tile_rows, tile_cols, tile_counts
):
    block_total = lax.axis_size("blk")
    copies = lax.axis_size("rep")
    replica = lax.axis_index("rep")
    width = out_grad.shape[1]
    side = tiles.shape[-1]
    slots_total = tiles.shape[2]
    share = jnp.dot(out_grad, w_neigh.T, preferred_element_type=jnp.float32).astype(jnp.bfloat16)
    whole = lax.all_gather(share, "rep", axis=0, tiled=True)
    block_rows = whole.shape[0]
    tiles_side = block_rows // side
    chunks_whole = whole.reshape(tiles_side, side, width)
    per_copy = (slots_total + copies - 1) // copies
    slot_ids = replica + copies * jnp.arange(per_copy, dtype=jnp.int32)
    valid = slot_ids < slots_total
    safe = jnp.minimum(slot_ids, slots_total - 1)
    wanted = jnp.take(tile_cols[0], safe, axis=1)
    found = chunks_whole[lax.all_to_all(wanted, "blk", split_axis=0, concat_axis=0, tiled=True)]
    fetched = lax.all_to_all(found, "blk", split_axis=0, concat_axis=0, tiled=True)
    chosen_tiles = jnp.take(tiles[0], safe, axis=1)
    products = jnp.einsum(
        "ikpq,ikqf->ikpf", chosen_tiles, fetched, preferred_element_type=jnp.float32
    )
    live = valid[None, :] & (slot_ids[None, :] < tile_counts[0][:, None])
    products = jnp.where(live[:, :, None, None], products, jnp.zeros_like(products))
    target_rows = jnp.take(tile_rows[0], safe, axis=1).reshape(-1)
    accumulated = jnp.zeros((tiles_side, side, width), jnp.float32)
    accumulated = accumulated.at[target_rows].add(products.reshape(-1, side, width))
    flat = accumulated.reshape(block_rows, width)
    self_part = jnp.dot(out_grad, w_self.T, preferred_element_type=jnp.float32)
    contract = (((0,), (0,)), ((), ()))
    terms_self = lax.dot_general(features, out_grad, contract, preferred_element_type=jnp.float32)
    terms_neigh = lax.dot_general(
        aggregated, out_grad, contract, preferred_element_type=jnp.float32
    )
    scale = (out_grad.shape[0] * block_total * copies) ** (-0.5)
    spread_share = lax.psum_scatter(flat, "rep", scatter_dimension=0, tiled=True)
    self_sum, neigh_sum = lax.psum((terms_self, terms_neigh), ("blk", "rep"))
    return (spread_share + self_part, self_sum * scale, neigh_sum * scale)


def solution(mesh):
    blocks, copies = mesh.shape["blk"], mesh.shape["rep"]
    by_pairs = copies == 2 and blocks % (CORES * ROWS_Y) == 0 and blocks > 2 * CORES * ROWS_Y
    placed = (
        P(("blk", "rep"), None),
        P(("blk", "rep"), None),
        P(("blk", "rep"), None),
        P(),
        P(),
        P("blk", None, None, None, None),
        P("blk", None, None),
        P("blk", None, None),
        P("blk", None),
    )
    return jax.shard_map(
        by_columns if by_pairs else on_device,
        mesh=mesh,
        in_specs=placed,
        out_specs=(P(("blk", "rep"), None), P(), P()),
        check_vma=False,
    )
```

```python
import functools

import jax
import jax.numpy as jnp
from jax import lax
from jax.experimental import pallas as pl
from jax.experimental.pallas import tpu as pltpu
from jax.sharding import PartitionSpec as P

MESH = pl.DeviceIdType.MESH
CORES, ROWS_Y = 2, 2


CHUNKS = 2


def schedule(line):
    last = line - 1
    own, across, ends, uses = {}, {}, {}, {}
    for h in range(CHUNKS):
        for w in range(2):
            across[0, w, h] = 1.1 + w + 0.01 * h
            own[1, w, h] = 1 + w + 0.01 * h
            across[1, w, h] = 4.05 + 0.5 * w + 0.01 * h
            for d in range(2, line):
                later = w + h if d == last else w + 1.05 * h
                own[d, w, h] = 2 * d - 1.5 + (later if w == 0 or d < last else 0.5 + 1.5 * h)
                across[d, w, h] = 2 * d + (h + 0.1 if d == last else 1.55 + 0.05 * w + (0.5 + 0.5 * w) * h)
        ends[1, h] = 3 + 0.01 * h
        for d in range(2, line):
            ends[d, h] = 2 * d + (h + 0.05 if d == last else 0.5 + 0.5 * h)
        for d in range(line):
            uses[d, 0, 0, h] = max(own[d, 1, h] if d else 1.0, 1.5) + 0.03
            uses[d, 1, 0, h] = (
                0.03
                + max(
                    [across[d, 0, h]]
                    + ([across[d, 1, h]] if d < last else [])
                    + ([ends[d, h]] if d else [])
                )
            )
            for other in range(2):
                when = uses[d, other, 0, h]
                uses[d, other, 1, h] = when + (0.45 if when < 2 * last else 0.1)
    return own, across, ends, uses


def layer_kernel(
    blocks,
    copies,
    scale,
    rows_ref,
    cols_ref,
    counts_ref,
    features_ref,
    aggregated_ref,
    grad_ref,
    w_self_ref,
    w_neigh_ref,
    tiles_ref,
    base_v,
    total,
    rows_v,
    counts_v,
    rows_s,
    cols_s,
    counts_s,
    features_v,
    aggregated_v,
    grad_v,
    w_self_v,
    w_neigh_v,
    tiles_v,
    g,
    across,
    current,
    chain,
    links_v,
    links_s,
    back,
    got,
    terms,
    from_core,
    half_sum,
    from_x,
    quarter_sum,
    from_plane,
    local_sem,
    send_sem,
    recv_sem,
    x_send,
    back_send,
    back_recv,
    core_send,
    core_recv,
    pair_send,
    pair_recv,
    plane_send,
    plane_recv,
):
    b = lax.axis_index("blk")
    r = lax.axis_index("rep")
    plane = CORES * ROWS_Y
    line = blocks // plane
    z, y, c = b // plane, (b // CORES) % ROWS_Y, b % CORES
    near_x = (b, 1 - r)
    near_core = (z * plane + y * CORES + (1 - c), r)
    near_y = (z * plane + (1 - y) * CORES + c, r)
    up, down = (b + plane, r), (b - plane, r)
    has_up, has_down = z < line - 1, z > 0
    never = z < 0
    always = z >= 0
    chunks, chunk_rows, width = g.shape[2:]
    slots, side = tiles_v.shape[1], tiles_v.shape[2]
    share_tiles = chunks * chunk_rows // side
    packed_tiles = chunk_rows // side
    of_lane = lax.broadcasted_iota(jnp.int32, (side, width), 1) // (width // chunks)
    seats = line * ROWS_Y
    seat = z * ROWS_Y + y
    end_of = lambda zz: (zz == 0) | (zz == line - 1)

    def local(src, dst, n):
        return pltpu.make_async_copy(src, dst, local_sem.at[n])

    loads = [
        local(grad_ref, grad_v, 0),
        local(w_neigh_ref, w_neigh_v, 1),
        local(features_ref, features_v, 2),
        local(aggregated_ref, aggregated_v, 3),
        local(rows_ref, rows_v, 4),
        local(counts_ref, counts_v, 5),
        local(rows_ref, rows_s, 6),
        local(cols_ref, cols_s, 7),
        local(counts_ref, counts_s, 8),
        local(w_self_ref, w_self_v, 9),
        local(tiles_ref, tiles_v, 10),
    ]
    for load in loads:
        load.start()

    barrier = pltpu.get_barrier_semaphore()

    def greet(device):
        pl.semaphore_signal(barrier, inc=1, device_id=device, device_id_type=MESH)

    def seat_device(step):
        other = (seat + step) % seats
        return other, ((other // ROWS_Y) * plane + (other % ROWS_Y) * CORES + c, r)

    greet(near_x)
    greet(near_core)

    @pl.loop(1, seats)
    def _(step):
        greet(seat_device(step)[1])

    loads[0].wait()
    loads[1].wait()

    features_each = width // chunks

    def message(which, h):
        first = pl.multiple_of(which * width + h * features_each, features_each)
        chosen = w_neigh_v[pl.ds(first, features_each), :]
        blank = jnp.zeros_like(chosen)
        packed = [
            lax.dot_general(
                grad_v[q * chunk_rows : (q + 1) * chunk_rows, :],
                jnp.concatenate([chosen if n == q else blank for n in range(chunks)], axis=0),
                (((1,), (1,)), ((), ())),
                preferred_element_type=jnp.float32,
            )
            for q in range(chunks)
        ]
        return sum(packed[1:], packed[0]).astype(g.dtype)

    for h in range(chunks):
        g[b, r, h] = message(r, h)
    for h in range(chunks):
        across[h] = message(1 - r, h)

    pl.semaphore_wait(barrier, 2 + seats - 1)

    def send(block, share, h, way, device):
        return pltpu.make_async_remote_copy(
            src_ref=g.at[block, share, h],
            dst_ref=g.at[block, share, h],
            send_sem=send_sem.at[way, block, share, h],
            recv_sem=recv_sem.at[block, share, h],
            device_id=device,
            device_id_type=MESH,
        )

    def x_copy(h):
        return pltpu.make_async_remote_copy(
            src_ref=across.at[h],
            dst_ref=g.at[b, r, h],
            send_sem=x_send.at[h],
            recv_sem=recv_sem.at[b, r, h],
            device_id=near_x,
            device_id_type=MESH,
        )

    def arrived(block, share, h):
        send(block, share, h, 3, near_core).wait_recv()

    def pass_on(block, share, h, go_up, go_down, go_y):
        @pl.when(go_up)
        def _():
            send(block, share, h, 0, up).start()

        @pl.when(go_down)
        def _():
            send(block, share, h, 1, down).start()

        @pl.when(go_y)
        def _():
            send(block, share, h, 2, near_y).start()

        send(block, share, h, 3, near_core).start()

    def share_of(which):
        return r if which == 0 else 1 - r

    def there(zz):
        return (zz >= 0) & (zz < line)

    def own_line(d, which, h):
        share = share_of(which)

        for sign in (-1, 1):
            zz = z + sign * d

            @pl.when(there(zz))
            def _():
                block = zz * plane + y * CORES + c
                arrived(block, share, h)
                pass_on(
                    block,
                    share,
                    h,
                    has_up if sign < 0 else never,
                    has_down if sign > 0 else never,
                    jnp.logical_not(end_of(zz)) if which else always,
                )

    def from_across(h):
        arrived(b, 1 - r, h)
        pass_on(b, 1 - r, h, has_up, has_down, always)

    def from_y(d, which, h):
        share = share_of(which)

        for sign in (-1, 1) if d else (0,):
            zz = z + sign * d
            wanted = there(zz)
            if which and d:
                wanted = wanted & jnp.logical_not(end_of(zz))

            @pl.when(wanted)
            def _():
                block = zz * plane + (1 - y) * CORES + c
                arrived(block, share, h)
                onward = which == 1 and d == 0
                pass_on(
                    block,
                    share,
                    h,
                    has_up & (z == 0) if onward else never,
                    has_down & (z == line - 1) if onward else never,
                    never,
                )

    def end_line(d, h):
        share = share_of(1)

        for sign in (-1, 1):
            zz = z + sign * d

            @pl.when(there(zz) & end_of(zz))
            def _():
                block = zz * plane + (1 - y) * CORES + c
                arrived(block, share, h)
                pass_on(
                    block,
                    share,
                    h,
                    has_up if sign < 0 else never,
                    has_down if sign > 0 else never,
                    never,
                )

    own_times, y_times, end_times, use_times = schedule(line)
    order = sorted(
        (group[:3] for group in use_times if group[3] == 0),
        key=lambda group: (use_times[(*group, 0)], group),
    )
    starts, count = {}, 0
    for group in order:
        starts[group] = count
        count += 2 if group[0] else 1
    nothing = count * slots

    def block_of(zz, other_y, other_core):
        yy = 1 - y if other_y else y
        cc = 1 - c if other_core else c
        return zz * plane + yy * CORES + cc

    def chain_links():
        for n in (4, 5, 6, 7, 8):
            loads[n].wait()
        slot = lax.broadcasted_iota(jnp.int32, rows_v.shape, 0)
        lane = lax.broadcasted_iota(jnp.int32, rows_v.shape, 1)
        wanted = jnp.where(slot < counts_v[...], rows_v[...], -2)
        candidates = [
            (starts[group] + i, group, sign)
            for group in order
            for i, sign in enumerate((-1, 1) if group[0] else (0,))
        ]
        own = slot
        found = []
        for index, (d, other_y, other_core), sign in candidates:
            zz = z + sign * d
            ok = there(zz)
            block = jnp.where(ok, block_of(zz, other_y, other_core), 0)
            own = jnp.where((lane == block) & ok, slot + index * slots, own)
            found.append((index * slots, block, ok))

        def step(k, carry):
            before, last = carry
            for first, block, ok in found:
                ok = ok & (k < counts_s[0, block])
                row = jnp.where(ok, rows_s[k, block], -1)
                key = first + k
                before = jnp.where((wanted == row) & (own > key), jnp.maximum(before, key), before)
                last = jnp.where(lane == row, jnp.maximum(last, key), last)
            return before, last

        none = jnp.full(rows_v.shape, -1, jnp.int32)
        before, last = lax.fori_loop(0, slots, step, (none, none))
        links_v[0] = jnp.where(before < 0, nothing, before)
        links_v[1] = jnp.where(last < 0, nothing, last)
        for h in range(chunks):
            chain[h, nothing] = jnp.zeros(chain.shape[2:], chain.dtype)

    def links_copy():
        return local(links_v, links_s, 11)

    def multiply(group, h):
        d, other_y, other_core = group
        first = starts[group]

        def one(i):
            zz = z + (2 * i - 1) * d

            @pl.when(there(zz))
            def _():
                block = block_of(zz, other_y, other_core)
                if other_core:
                    for share in range(copies):
                        arrived(block, share, h)

                seat_of = first + i
                for share in range(copies):
                    current[h, seat_of, share] = g[block, share, h].reshape(current.shape[3:])
                products = []
                for k in range(slots):
                    column = cols_s[k, block]
                    share, within = column // share_tiles, column % share_tiles
                    piece = current[h, seat_of, share, within % packed_tiles]
                    piece = jnp.where(of_lane == within // packed_tiles, piece, jnp.zeros_like(piece))
                    products.append(
                        jnp.dot(tiles_v[block, k], piece, preferred_element_type=jnp.float32)
                    )
                for k in range(slots):
                    chain[h, seat_of * slots + k] = products[k] + chain[h, links_s[0, k, block]]

        if d:

            @pl.loop(0, 2)
            def _(i):
                one(i)
        else:
            one(0)

    out_width = total.shape[1]
    half, quarter = total.shape[0] // 2, total.shape[0] // 4
    first_owner, owners = (ROWS_Y, seats - 2 * ROWS_Y) if line > 2 else (0, seats)
    part = quarter // owners
    owns = (seat >= first_owner) & (seat < first_owner + owners)

    def core_copy():
        return pltpu.make_async_remote_copy(
            src_ref=terms.at[pl.ds((1 - c) * half, half)],
            dst_ref=from_core,
            send_sem=core_send.at[0],
            recv_sem=core_recv.at[0],
            device_id=near_core,
            device_id_type=MESH,
        )

    def pair_copy():
        return pltpu.make_async_remote_copy(
            src_ref=half_sum.at[pl.ds((1 - r) * quarter, quarter)],
            dst_ref=from_x,
            send_sem=pair_send.at[0],
            recv_sem=pair_recv.at[0],
            device_id=near_x,
            device_id_type=MESH,
        )

    def part_of(owner):
        return pl.multiple_of((owner - first_owner) * part, part)

    def part_copy(owner, slot):
        return pltpu.make_async_remote_copy(
            src_ref=quarter_sum.at[pl.ds(part_of(owner), part)],
            dst_ref=from_plane.at[slot],
            send_sem=plane_send.at[0, owner],
            recv_sem=plane_recv.at[0, slot],
            device_id=seat_device(owner - seat + seats)[1],
            device_id_type=MESH,
        )

    def others(first, count, act):
        @pl.loop(first, first + count)
        def _(other):
            @pl.when(other != seat)
            def _():
                act(other)

    def share_copy(other, owner):
        device = seat_device(other - seat + seats)[1]
        where = pl.ds(c * half + r * quarter + part_of(owner), part)
        return pltpu.make_async_remote_copy(
            src_ref=total.at[where],
            dst_ref=total.at[where],
            send_sem=plane_send.at[1, other],
            recv_sem=plane_recv.at[1, owner],
            device_id=device,
            device_id_type=MESH,
        )

    def pair_back(rr):
        where = pl.ds(c * half + rr * quarter, quarter)
        return pltpu.make_async_remote_copy(
            src_ref=total.at[where],
            dst_ref=total.at[where],
            send_sem=pair_send.at[1],
            recv_sem=pair_recv.at[1],
            device_id=near_x,
            device_id_type=MESH,
        )

    def core_back(cc):
        where = pl.ds(cc * half, half)
        return pltpu.make_async_remote_copy(
            src_ref=total.at[where],
            dst_ref=total.at[where],
            send_sem=core_send.at[1],
            recv_sem=core_recv.at[1],
            device_id=near_core,
            device_id_type=MESH,
        )

    def make_terms():
        loads[2].wait()
        loads[3].wait()
        for n, operand in enumerate((features_v, aggregated_v)):
            terms[n * half : (n + 1) * half, :] = lax.dot_general(
                operand[...],
                grad_v[...],
                (((0,), (0,)), ((), ())),
                preferred_element_type=jnp.float32,
            )
        core_copy().start()

    def over_cores():
        core_copy().wait_recv()
        half_sum[...] = terms[pl.ds(pl.multiple_of(c * half, half), half), :] + from_core[...]
        pair_copy().start()

    def over_pair():
        pair_copy().wait_recv()
        quarter_sum[...] = (
            half_sum[pl.ds(pl.multiple_of(r * quarter, quarter), quarter), :] + from_x[...]
        )

        others(first_owner, owners, lambda other: part_copy(other, seat).start())

    def over_plane():
        @pl.when(owns)
        def _():
            from_plane[seat] = quarter_sum[pl.ds(part_of(seat), part), :]
            others(0, seats, lambda other: part_copy(seat, other).wait_recv())
            where = pl.ds(pl.multiple_of(c * half + r * quarter + part_of(seat), part), part)
            total[where, :] = jnp.sum(from_plane[...], axis=0) * scale
            others(0, seats, lambda other: share_copy(other, seat).start())

    def back_over_pair():
        others(first_owner, owners, lambda other: share_copy(seat, other).wait_recv())
        pair_back(r).start()

    def back_over_cores():
        pair_back(1 - r).wait_recv()
        core_back(c).start()

    def self_part():
        loads[9].wait()

        @pl.loop(0, chunks)
        def _(h):
            where = pl.ds(pl.multiple_of(h * chunk_rows, chunk_rows), chunk_rows)
            base_v[where, :] = lax.dot_general(
                grad_v[where, :],
                w_self_v[...],
                (((1,), (1,)), ((), ())),
                preferred_element_type=jnp.float32,
            )

    for h in range(chunks):
        x_copy(h).start()
        pass_on(b, r, h, has_up, has_down, always)

    def back_copy(h):
        return pltpu.make_async_remote_copy(
            src_ref=back.at[h],
            dst_ref=got.at[h],
            send_sem=back_send.at[h],
            recv_sem=back_recv.at[h],
            device_id=near_x,
            device_id_type=MESH,
        )

    own_half = pl.ds(pl.multiple_of(r * width, width), width)
    other_half = pl.ds(pl.multiple_of((1 - r) * width, width), width)

    def turned(value):
        return pltpu.roll(value, width // chunks, 1)

    def whole(h, row):
        value = chain[h, links_s[1, 0, row]]
        return value + turned(value)

    def give_back(h):
        for t in range(packed_tiles):
            row = (1 - r) * share_tiles + t
            low, high = whole(h, row), whole(h, row + packed_tiles)
            back[h, t * side : (t + 1) * side, :] = jnp.where(of_lane == 0, low, high).astype(
                back.dtype
            )

    def keep(h):
        for t in range(share_tiles):
            if t == 1:
                back_copy(h).start()
            value = whole(h, r * share_tiles + t)
            value = jnp.where(of_lane == h, value, jnp.zeros_like(value))
            base_v[t * side : (t + 1) * side, own_half] += value

    def take(h):
        back_copy(h).wait_recv()
        for t in range(packed_tiles):
            value = got[h, t * side : (t + 1) * side, :].astype(jnp.float32)
            other = turned(value)
            for q in range(chunks):
                chosen = value if q == h else other
                chosen = jnp.where(of_lane == h, chosen, jnp.zeros_like(chosen))
                first = (t + q * packed_tiles) * side
                base_v[first : first + side, other_half] += chosen

    events = [
        (0.1, make_terms),
        (1.2, chain_links),
        (1.25, lambda: links_copy().start()),
        (1.15, over_cores),
        (1.45, lambda: (links_copy().wait(), loads[10].wait())),
        (1.9, over_pair),
        (2.9, self_part),
        (3.9, over_plane),
        (5.9, back_over_pair),
        (6.65, back_over_cores),
    ]
    for h in range(chunks):
        events.append((1.0 + 0.01 * h, functools.partial(from_across, h)))
    for act, times in ((own_line, own_times), (from_y, y_times), (end_line, end_times)):
        for key, when in times.items():
            if act is not from_y or key[:2] != (line - 1, 1):
                events.append((when, functools.partial(act, *key)))
    for h in range(chunks):
        when = 0
        for group in order:
            when = max(when, use_times[(*group, h)])
            events.append((when, functools.partial(multiply, group, h)))
        events.append((when + 0.001, functools.partial(give_back, h)))
        events.append((when + 0.002, functools.partial(keep, h)))
    for _, event in sorted(events, key=lambda pair: pair[0]):
        event()

    for h in range(chunks - 1):
        take(h)
    core_back(1 - c).wait_recv()

    core_copy().wait_send()
    pair_copy().wait_send()
    pair_back(r).wait_send()
    core_back(c).wait_send()

    others(first_owner, owners, lambda other: part_copy(other, seat).wait_send())

    @pl.when(owns)
    def _():
        others(0, seats, lambda other: share_copy(other, seat).wait_send())

    @pl.loop(0, chunks)
    def _(h):
        x_copy(h).wait_send()

        @pl.loop(0, line)
        def _(zz):
            for which in range(2):
                share = share_of(which)
                block = zz * plane + y * CORES + c
                beyond = zz * plane + (1 - y) * CORES + c
                special = end_of(zz) if which else never
                goes_up = (zz <= z) & has_up
                goes_down = (zz >= z) & has_down

                @pl.when(goes_up)
                def _():
                    send(block, share, h, 0, up).wait_send()

                @pl.when(goes_down)
                def _():
                    send(block, share, h, 1, down).wait_send()

                @pl.when(jnp.logical_not(special) | (zz == z))
                def _():
                    send(block, share, h, 2, near_y).wait_send()

                send(block, share, h, 3, near_core).wait_send()

                @pl.when(special & goes_up)
                def _():
                    send(beyond, share, h, 0, up).wait_send()

                @pl.when(special & goes_down)
                def _():
                    send(beyond, share, h, 1, down).wait_send()

                send(beyond, share, h, 3, near_core).wait_send()

    for h in range(chunks):
        back_copy(h).wait_send()
    take(chunks - 1)


def layer(rows, cols, counts, features, aggregated, grad, w_self, w_neigh, tiles, scale, blocks, copies):
    share_rows, width = grad.shape
    half = width // copies
    _, slots, side, _ = tiles.shape
    line = blocks // (CORES * ROWS_Y)
    seats = line * ROWS_Y
    chunk_rows = share_rows // CHUNKS
    owners = seats - 2 * ROWS_Y if line > 2 else seats
    count = 2 * CORES * (2 * line - 1)
    bf16, f32, i32 = jnp.bfloat16, jnp.float32, jnp.int32
    dma = pltpu.SemaphoreType.DMA
    operands = (rows, cols, counts, features, aggregated, grad, w_self, w_neigh, tiles)
    return pl.pallas_call(
        functools.partial(layer_kernel, blocks, copies, scale),
        out_shape=(
            pltpu.VMEM((share_rows, width), f32),
            pltpu.VMEM((2 * width, width), f32),
        ),
        in_specs=[pl.BlockSpec(memory_space=pl.ANY)] * 9,
        out_specs=(
            pl.BlockSpec(memory_space=pltpu.VMEM),
            pl.BlockSpec(memory_space=pltpu.VMEM),
        ),
        scratch_shapes=[
            pltpu.VMEM(rows.shape, i32),
            pltpu.VMEM(counts.shape, i32),
            pltpu.SMEM(rows.shape, i32),
            pltpu.SMEM(cols.shape, i32),
            pltpu.SMEM(counts.shape, i32),
            pltpu.VMEM(features.shape, bf16),
            pltpu.VMEM(aggregated.shape, bf16),
            pltpu.VMEM(grad.shape, bf16),
            pltpu.VMEM(w_self.shape, bf16),
            pltpu.VMEM(w_neigh.shape, bf16),
            pltpu.VMEM(tiles.shape, bf16),
            pltpu.VMEM((blocks, copies, CHUNKS, chunk_rows, half), bf16),
            pltpu.VMEM((CHUNKS, chunk_rows, half), bf16),
            pltpu.VMEM((CHUNKS, count, copies, chunk_rows // side, side, half), bf16),
            pltpu.VMEM((CHUNKS, count * slots + 1, side, half), f32),
            pltpu.VMEM((2, *rows.shape), i32),
            pltpu.SMEM((2, *rows.shape), i32),
            pltpu.VMEM((CHUNKS, chunk_rows, half), bf16),
            pltpu.VMEM((CHUNKS, chunk_rows, half), bf16),
            pltpu.VMEM((2 * width, width), f32),
            pltpu.VMEM((width, width), f32),
            pltpu.VMEM((width, width), f32),
            pltpu.VMEM((width // 2, width), f32),
            pltpu.VMEM((width // 2, width), f32),
            pltpu.VMEM((seats, width // 2 // owners, width), f32),
            dma((12,)),
            dma((4, blocks, copies, CHUNKS)),
            dma((blocks, copies, CHUNKS)),
            dma((CHUNKS,)),
            dma((CHUNKS,)),
            dma((CHUNKS,)),
            dma((2,)),
            dma((2,)),
            dma((2,)),
            dma((2,)),
            dma((2, seats)),
            dma((2, seats)),
        ],
        compiler_params=pltpu.CompilerParams(collective_id=0, has_side_effects=True, vmem_limit_bytes=60 << 20),
    )(*(pltpu.with_memory_space_constraint(operand, pltpu.HBM) for operand in operands))


def finish_kernel(grad_ref, sums_ref, *refs):
    outs, sem = refs[:3], refs[3]
    width = sums_ref.shape[1]
    sources = (grad_ref, sums_ref.at[pl.ds(0, width)], sums_ref.at[pl.ds(width, width)])
    copies = [
        pltpu.make_async_copy(src, dst, sem.at[n]) for n, (src, dst) in enumerate(zip(sources, outs))
    ]
    for copy in copies:
        copy.start()
    for copy in copies:
        copy.wait()


def finish(feature_grad, sums):
    width = sums.shape[1]
    square = jax.ShapeDtypeStruct((width, width), sums.dtype)
    return pl.pallas_call(
        finish_kernel,
        out_shape=(jax.ShapeDtypeStruct(feature_grad.shape, feature_grad.dtype), square, square),
        in_specs=[pl.BlockSpec(memory_space=pl.ANY)] * 2,
        out_specs=(pl.BlockSpec(memory_space=pl.ANY),) * 3,
        scratch_shapes=[pltpu.SemaphoreType.DMA((3,))],
        compiler_params=pltpu.CompilerParams(vmem_limit_bytes=1 << 20),
    )(feature_grad, sums)


def by_columns(
    features, aggregated, out_grad, w_self, w_neigh, tiles, tile_rows, tile_cols, tile_counts
):
    blocks, copies = lax.axis_size("blk"), lax.axis_size("rep")
    rows, width = out_grad.shape
    scale = (rows * blocks * copies) ** (-0.5)
    feature_grad, sums = layer(
        tile_rows[0].T,
        tile_cols[0].T,
        tile_counts,
        features,
        aggregated,
        out_grad,
        w_self,
        w_neigh,
        tiles[0],
        scale,
        blocks,
        copies,
    )
    return finish(feature_grad, sums)


def on_device(
    features, aggregated, out_grad, w_self, w_neigh, tiles, tile_rows, tile_cols, tile_counts
):
    block_total = lax.axis_size("blk")
    copies = lax.axis_size("rep")
    replica = lax.axis_index("rep")
    width = out_grad.shape[1]
    side = tiles.shape[-1]
    slots_total = tiles.shape[2]
    share = jnp.dot(out_grad, w_neigh.T, preferred_element_type=jnp.float32).astype(jnp.bfloat16)
    whole = lax.all_gather(share, "rep", axis=0, tiled=True)
    block_rows = whole.shape[0]
    tiles_side = block_rows // side
    chunks_whole = whole.reshape(tiles_side, side, width)
    per_copy = (slots_total + copies - 1) // copies
    slot_ids = replica + copies * jnp.arange(per_copy, dtype=jnp.int32)
    valid = slot_ids < slots_total
    safe = jnp.minimum(slot_ids, slots_total - 1)
    wanted = jnp.take(tile_cols[0], safe, axis=1)
    found = chunks_whole[lax.all_to_all(wanted, "blk", split_axis=0, concat_axis=0, tiled=True)]
    fetched = lax.all_to_all(found, "blk", split_axis=0, concat_axis=0, tiled=True)
    chosen_tiles = jnp.take(tiles[0], safe, axis=1)
    products = jnp.einsum(
        "ikpq,ikqf->ikpf", chosen_tiles, fetched, preferred_element_type=jnp.float32
    )
    live = valid[None, :] & (slot_ids[None, :] < tile_counts[0][:, None])
    products = jnp.where(live[:, :, None, None], products, jnp.zeros_like(products))
    target_rows = jnp.take(tile_rows[0], safe, axis=1).reshape(-1)
    accumulated = jnp.zeros((tiles_side, side, width), jnp.float32)
    accumulated = accumulated.at[target_rows].add(products.reshape(-1, side, width))
    flat = accumulated.reshape(block_rows, width)
    self_part = jnp.dot(out_grad, w_self.T, preferred_element_type=jnp.float32)
    contract = (((0,), (0,)), ((), ()))
    terms_self = lax.dot_general(features, out_grad, contract, preferred_element_type=jnp.float32)
    terms_neigh = lax.dot_general(
        aggregated, out_grad, contract, preferred_element_type=jnp.float32
    )
    scale = (out_grad.shape[0] * block_total * copies) ** (-0.5)
    spread_share = lax.psum_scatter(flat, "rep", scatter_dimension=0, tiled=True)
    self_sum, neigh_sum = lax.psum((terms_self, terms_neigh), ("blk", "rep"))
    return (spread_share + self_part, self_sum * scale, neigh_sum * scale)


def solution(mesh):
    blocks, copies = mesh.shape["blk"], mesh.shape["rep"]
    by_pairs = copies == 2 and blocks % (CORES * ROWS_Y) == 0 and blocks > 2 * CORES * ROWS_Y
    placed = (
        P(("blk", "rep"), None),
        P(("blk", "rep"), None),
        P(("blk", "rep"), None),
        P(),
        P(),
        P("blk", None, None, None, None),
        P("blk", None, None),
        P("blk", None, None),
        P("blk", None),
    )
    return jax.shard_map(
        by_columns if by_pairs else on_device,
        mesh=mesh,
        in_specs=placed,
        out_specs=(P(("blk", "rep"), None), P(), P()),
        check_vma=False,
    )
```
